256 devices in a mesh: dp: 16 (over y, z_hi, core), pool: 16 (over x, z_lo).
Axes of the slice: x: 4, y: 4, z: 8 (z_hi: 2, z_lo: 4; z = z_hi * 4 + z_lo), core: 2. Of those that a mesh axis runs over, the one named last changes fastest.
Arguments:
- feats: bfloat16 [65536, 2048], P(('dp', 'pool')), may hold values from -24 to 24
- tower_w: bfloat16 [2048, 256], replicated, may hold values from -0.125 to 0.125
- partners: int32 [65536], P(('dp', 'pool')), may hold values from 0 to 4095, as said below
- popularity_buckets: int32 [65536], P(('dp', 'pool')), may hold values from 0 to 31
- row_counts: int32 [16, 16], replicated, may hold values from 64 to 256, as said below
Outputs:
- grad_w: float32 [2048, 256], P(('dp', 'pool'))
The draws below stay inside these ranges and needn't reach their ends.
Inputs may be any that keep to these rules, and one draw needn't show every extreme that they name: row_counts[d, p] valid slots stand first in the block of 256 slots of pool member p in data group d; in every data group some member has all 256 slots valid. `partners`: each slot's partner is the position, within its data group's 4096 slots, of a valid slot other than itself.
All inputs are finite; a program needn't handle non-finite values.
Results may differ from the reference program's by a relative error of at most 0.0038.
The reference program's roundings to bfloat16 on the way count: a program that leaves them out, or rounds other values in their place, can miss the bound.
Values may be sent and summed in bfloat16 or wider, within the bound.
A program may use at most 64 MiB of HBM per device.

```python
import jax
import jax.numpy as jnp
from jax import lax

DIN = 2048
DE = 256
ROWS_DEV = 256
NBINS = 32
VIEWS = 4096
ROWS = 65536
N_DP = 16
N_POOL = 16


def tally_matrix(key):
    base_key = jax.random.fold_in(key, 7001)
    lowest = ROWS_DEV // 4
    counts = jax.random.randint(jax.random.fold_in(base_key, 1), (N_DP, N_POOL), lowest, ROWS_DEV + 1)
    full_at = jax.random.randint(jax.random.fold_in(base_key, 2), (N_DP,), 0, N_POOL)
    full_at = jnp.where(jnp.arange(N_DP) == 0, N_POOL - 1, full_at)
    members = jnp.arange(N_POOL)[None, :]
    counts = jnp.where(members == full_at[:, None], ROWS_DEV, counts)
    empty_at = (full_at[0] + 1) % N_POOL
    first_group = jnp.arange(N_DP)[:, None] == 0
    counts = jnp.where(first_group & (members == empty_at), lowest, counts)
    return counts.astype(jnp.int32)


def draw_row_counts(key, part):
    return tally_matrix(key)


def draw_partners(key, part):
    counts = tally_matrix(key)
    base_key = jax.random.fold_in(key, 7002)
    owner_index = jax.random.randint(jax.random.fold_in(base_key, 1), (N_DP, VIEWS), 0, N_POOL)
    available = jnp.take_along_axis(counts, owner_index, axis=1)
    raw_bits = jax.random.randint(jax.random.fold_in(base_key, 2), (N_DP, VIEWS), 0, 1 << 30)
    local_row = raw_bits % available
    picked = owner_index * ROWS_DEV + local_row
    own_index = jnp.arange(VIEWS)[None, :]
    picked = jnp.where(picked == own_index, owner_index * ROWS_DEV + (local_row + 1) % available, picked)
    group_rows = jnp.arange(N_DP)[:, None]
    picked = jnp.where((group_rows == 0) & (own_index == 0), VIEWS - 1, picked)
    picked = jnp.where((group_rows == 0) & (own_index == VIEWS - 1), 0, picked)
    return picked.reshape(N_DP * VIEWS).astype(jnp.int32)


def set_ends(result, stream_key, least, high):
    extent = result.shape
    index_at = [jax.random.randint(jax.random.fold_in(stream_key, axis), (), 0, extent[axis]) for axis in range(len(extent))]
    result = result.at[tuple(index_at)].set(least)
    longest = extent.index(max(extent))
    index_at[longest] = (index_at[longest] + 1) % extent[longest]
    return result.at[tuple(index_at)].set(high)


def raised(entries, key, source, target, blocks, factor):
    def block_of(axis_at):
        return (jnp.arange(entries.shape[axis_at]) // (entries.shape[axis_at] // blocks)).reshape((-1,) + (1,) * (entries.ndim - 1 - axis_at))

    one_side = jax.random.permutation(key, blocks)[block_of(target)]
    second = (block_of(target) + blocks // 2) % blocks
    return jnp.where((block_of(source) == one_side) | (block_of(source) == second), factor * entries, entries)


def block_levels(stream_key, dims, split, least, high):
    def one(axis_at, blocks):
        steps = jax.random.uniform(jax.random.fold_in(jax.random.fold_in(stream_key, 6), axis_at), (blocks,), jnp.float32, least / len(split), high / len(split))
        return jnp.repeat(jnp.exp(steps), dims[axis_at] // blocks).reshape((-1,) + (1,) * (len(dims) - axis_at - 1))

    gain = one(*split[0])
    for cut in split[1:]:
        gain = gain * one(*cut)
    return gain


def scatter_about(rng, shape, spread, most, shards=(), kind=jnp.bfloat16):
    values = spread * jax.random.normal(rng, shape, jnp.float32)
    if shards:
        values = values * block_levels(rng, shape, shards, -0.22, 0.18)
    return jnp.clip(values, -most, most).astype(kind)


def heavy_noise(own_key, shape, deviation, most, cuts, heavy, held_as=jnp.bfloat16):
    array = deviation * jax.random.normal(own_key, shape, jnp.float32)
    if cuts:
        array = array * block_levels(own_key, shape, cuts, -0.22, 0.18)
    return jnp.clip(raised(array, jax.random.fold_in(own_key, 3), *heavy), -most, most).astype(held_as)


def setup_inputs(seed: int = 0) -> dict:
    streams_of = jax.random.split(jax.random.key(seed), 6)
    return {
        "feats": heavy_noise(streams_of[0], (ROWS, DIN), 1.0, 24.0, ((0, 256),), (0, 1, 256, 6.0)),
        "tower_w": scatter_about(streams_of[1], (DIN, DE), DIN ** -0.5, 0.125),
        "partners": draw_partners(jax.random.fold_in(streams_of[5], 71), 0),
        "popularity_buckets": set_ends(jax.random.randint(streams_of[3], (ROWS,), 0, NBINS), jax.random.fold_in(streams_of[3], 1), 0, NBINS - 1).astype(jnp.int32),
        "row_counts": draw_row_counts(jax.random.fold_in(streams_of[5], 71), 0),
    }


sharpness_scaler = 0.05
epsilon = 1e-06

def group_grad(embedded, prior_occurrence_correction, partners, perspective_usable):
    group_rows = embedded.shape[0]
    emb_float = embedded.astype(jnp.float32)
    angular_affinities = jnp.dot(emb_float, emb_float.T, preferred_element_type=jnp.float32)
    position = jnp.arange(group_rows, dtype=jnp.int32)
    admitted_flags = perspective_usable[None, :] & (position[:, None] != position[None, :])
    natural_powers = jnp.where(admitted_flags, jnp.exp(angular_affinities / sharpness_scaler - prior_occurrence_correction.astype(jnp.float32)[None, :]), 0.0)
    normalizer_sums = lax.optimization_barrier(jnp.sum(natural_powers, axis=1, keepdims=True))
    matched_partner = (partners[:, None] == position[None, :]).astype(jnp.float32)
    pair_multiplier = jnp.where(perspective_usable[:, None], natural_powers / normalizer_sums - matched_partner, 0.0).astype(jnp.bfloat16)
    pair_multiplier = lax.optimization_barrier(pair_multiplier).astype(jnp.float32)
    return jnp.dot(pair_multiplier, emb_float, preferred_element_type=jnp.float32) + jnp.dot(pair_multiplier.T, emb_float, preferred_element_type=jnp.float32)

def reference(feats, tower_w, partners, popularity_buckets, row_counts):
    projected = jnp.dot(feats, tower_w, preferred_element_type=jnp.float32)
    inv_norm = lax.rsqrt(lax.optimization_barrier(jnp.sum(projected * projected, axis=1, keepdims=True)) + epsilon)
    normed = projected * inv_norm
    embedded = normed.astype(jnp.bfloat16)
    prior_occurrence_correction = (-(popularity_buckets.astype(jnp.float32) + 0.5) / 4.0).astype(jnp.bfloat16)
    position_index = jnp.arange(VIEWS, dtype=jnp.int32) % ROWS_DEV
    owner_index = jnp.arange(VIEWS, dtype=jnp.int32) // ROWS_DEV
    perspective_usable = position_index[None, :] < row_counts[:, owner_index]
    packed = (embedded.reshape(N_DP, VIEWS, DE), prior_occurrence_correction.reshape(N_DP, VIEWS), partners.reshape(N_DP, VIEWS), perspective_usable)
    group_grads = lax.map(lambda operand_tensors: group_grad(*operand_tensors), packed)
    grad_emb = group_grads.reshape(ROWS, DE)
    grad_proj = ((grad_emb - normed * lax.optimization_barrier(jnp.sum(normed * grad_emb, axis=1, keepdims=True))) * inv_norm).astype(jnp.bfloat16)
    return lax.dot_general(feats, grad_proj, (((0,), (0,)), ((), ())), preferred_element_type=jnp.float32)
```

```python
import functools

import jax
import jax.numpy as jnp
from jax import lax
from jax.experimental import pallas as pl
from jax.experimental.pallas import tpu as pltpu
from jax.sharding import PartitionSpec as P

MESH = pl.DeviceIdType.MESH
EPS = 1e-06
SCALE = 28.853900817779268
ROWS = 256
HALF = 128
DE = 256
DIN = 2048
KC = 4
KW = DIN // KC


def nt(left, right):
    return lax.dot_general(
        left, right, (((1,), (1,)), ((), ())), preferred_element_type=jnp.float32
    )


def nn(left, right):
    return jnp.dot(left, right, preferred_element_type=jnp.float32)


def kernel(
    feats_hbm, w_hbm, part_ref, buck_ref, counts_ref, out_ref,
    feats_v, w_v, feats_t, e_all, p_all, meta, recips,
    normed_s, inv_s, own_w, own_part, own_valid, tot_s, g_s,
    core_send, core_recv, send2, recv2, acc2, send3, recv3, send4, recv4,
    in_sem, meta_ssem, meta_rsem, e_ssem, e_rsem, r_ssem, r_rsem,
    c_ssem, c_rsem, s2_sem, r2_sem, s3_sem, r3_sem, s4_sem, r4_sem,
):
    dp = lax.axis_index("dp")
    pool = lax.axis_index("pool")
    y = dp // 4
    zh = (dp // 2) % 2
    core = dp % 2
    x = pool // 4
    z = pool % 4

    loads = []
    for k in range(KC):
        cols = pl.ds(k * KW, KW)
        a = pltpu.make_async_copy(feats_hbm.at[:, cols], feats_v.at[:, cols], in_sem.at[k, 0])
        b = pltpu.make_async_copy(w_hbm.at[cols, :], w_v.at[cols, :], in_sem.at[k, 1])
        a.start()
        b.start()
        loads.append((a, b))

    barrier = pltpu.get_barrier_semaphore()

    def greet(d, p):
        pl.semaphore_signal(barrier, inc=1, device_id=(d, p), device_id_type=MESH)

    for k in range(1, 16):
        greet(dp, (pool + k) % 16)
    greet(y * 4 + zh * 2 + (1 - core), pool)
    for k in range(1, 4):
        greet(((y + k) % 4) * 4 + zh * 2 + core, pool)
    for k in range(4):
        greet(y * 4 + (1 - zh) * 2 + core, x * 4 + k)

    cnt = counts_ref[dp, pool]
    lane = lax.broadcasted_iota(jnp.int32, (1, ROWS), 1)
    valid = lane < cnt
    part_l = jnp.where(valid, part_ref[...], -1).astype(jnp.float32)
    w_l = jnp.where(valid, jnp.exp((buck_ref[...].astype(jnp.float32) + 0.5) * 0.25), 0.0)
    meta[pool, 0:1, :] = part_l
    meta[pool, 1:2, :] = w_l
    own_part[...] = jnp.broadcast_to(part_l, (128, ROWS)).T
    own_w[...] = jnp.broadcast_to(w_l, (128, ROWS)).T
    own_valid[...] = jnp.broadcast_to(jnp.where(valid, 1.0, 0.0), (128, ROWS)).T

    projected = None
    for k in range(KC):
        loads[k][0].wait()
        loads[k][1].wait()
        cols = pl.ds(k * KW, KW)
        term = nn(feats_v[:, cols], w_v[cols, :])
        projected = term if projected is None else projected + term
    inv_norm = lax.rsqrt(jnp.sum(projected * projected, axis=1, keepdims=True) + EPS)
    normed = projected * inv_norm
    normed_s[...] = normed
    inv_s[...] = jnp.broadcast_to(inv_norm, (ROWS, 128))
    e_all[pool] = normed.astype(jnp.bfloat16)

    pl.semaphore_wait(barrier, 23)

    pending = []
    for k in range(1, 16):
        c = pltpu.make_async_remote_copy(
            src_ref=meta.at[pool], dst_ref=meta.at[pool],
            send_sem=meta_ssem.at[k], recv_sem=meta_rsem.at[pool],
            device_id=(dp, (pool + k) % 16), device_id_type=MESH,
        )
        c.start()
        pending.append(c)

    def rows_of(h):
        return pl.ds(h * HALF, HALF)

    def send(slot, h, target, n):
        c = pltpu.make_async_remote_copy(
            src_ref=e_all.at[slot, rows_of(h)], dst_ref=e_all.at[slot, rows_of(h)],
            send_sem=e_ssem.at[n], recv_sem=e_rsem.at[slot, h],
            device_id=(dp, target), device_id_type=MESH,
        )
        c.start()
        pending.append(c)

    def arrive(slot, h):
        pltpu.make_async_remote_copy(
            src_ref=e_all.at[slot, rows_of(h)], dst_ref=e_all.at[slot, rows_of(h)],
            send_sem=e_ssem.at[0], recv_sem=e_rsem.at[slot, h],
            device_id=(dp, pool), device_id_type=MESH,
        ).wait_recv()

    def meta_arrive(slot):
        pltpu.make_async_remote_copy(
            src_ref=meta.at[slot], dst_ref=meta.at[slot],
            send_sem=meta_ssem.at[0], recv_sem=meta_rsem.at[slot],
            device_id=(dp, pool), device_id_type=MESH,
        ).wait_recv()

    zs = [z, z + 1 - 2 * (z % 2), (z + 2) % 4, 3 - z]
    right = (x + 1) % 4
    left = (x + 3) % 4
    far = (x + 2) % 4
    count = iter(range(64))

    def spread(slot, halves):
        for h in halves:
            send(slot, h, right * 4 + z, next(count))
            send(slot, 1 - h, left * 4 + z, next(count))

    spread(pool, (0, 1))
    for c in (1, 2, 3):
        for h in (0, 1):
            send(pool, h, x * 4 + zs[c], next(count))

    def scores(slot, first=False):
        s = nt(e_all[pool], e_all[slot])
        e = jnp.exp2(s * SCALE)
        if first:
            ri = lax.broadcasted_iota(jnp.int32, (ROWS, ROWS), 0)
            ci = lax.broadcasted_iota(jnp.int32, (ROWS, ROWS), 1)
            e = jnp.where(ri == ci, 0.0, e)
        p_all[slot] = e
        t = e * meta[slot, 1:2, :]
        t = t[:, :128] + t[:, 128:]
        if first:
            tot_s[...] = t
        else:
            tot_s[...] += t

    scores(pool, True)

    def transposes(lo, hi):
        for m in range(lo, hi):
            my, mz, mc = m // 4, (m // 2) % 2, m % 2
            t = feats_v[:, m * 128:(m + 1) * 128].T
            which = (mc + core) % 2
            for mx in range(4):
                at = (my * (8 - 6 * mc) + mx * (2 + 6 * mc) + mz) * 32
                feats_t[which, at:at + 32, :] = t[mx * 32:(mx + 1) * 32]

    transposes(0, 8)

    for c in range(4):
        if c < 3:
            nslot = x * 4 + zs[c + 1]
            for h in (0, 1):
                arrive(nslot, h)
                send(nslot, h, right * 4 + z, next(count))
                send(nslot, h, left * 4 + z, next(count))
        ls = left * 4 + zs[c]
        rs = right * 4 + zs[c]
        arrive(ls, 0)
        send(ls, 0, right * 4 + z, next(count))
        arrive(rs, 1)
        send(rs, 1, left * 4 + z, next(count))
        if c == 0:
            transposes(8, 16)
        if c < 3:
            meta_arrive(nslot)
            scores(nslot)
        arrive(ls, 1)
        meta_arrive(ls)
        scores(ls)
        arrive(rs, 0)
        meta_arrive(rs)
        scores(rs)
        if c > 0:
            fs = far * 4 + zs[c - 1]
            arrive(fs, 0)
            arrive(fs, 1)
            meta_arrive(fs)
            scores(fs)
    fs = far * 4 + zs[3]
    arrive(fs, 0)
    arrive(fs, 1)
    meta_arrive(fs)
    scores(fs)

    total = jnp.broadcast_to(jnp.sum(tot_s[...], axis=1, keepdims=True), (ROWS, 128))
    recip_own = own_valid[...] / total
    recips[pool] = recip_own.T[0:1, :]
    for k in range(1, 16):
        c = pltpu.make_async_remote_copy(
            src_ref=recips.at[pool], dst_ref=recips.at[pool],
            send_sem=r_ssem.at[k], recv_sem=r_rsem.at[pool],
            device_id=(dp, (pool + k) % 16), device_id_type=MESH,
        )
        c.start()
        pending.append(c)

    wide = lambda v: jnp.concatenate([v, v], axis=1)
    tot_s[...] = recip_own
    g_s[...] = jnp.zeros_like(g_s)
    lane_f = lax.broadcasted_iota(jnp.int32, (ROWS, ROWS), 1).astype(jnp.float32)
    row_f = lax.broadcasted_iota(jnp.int32, (ROWS, ROWS), 0).astype(jnp.float32)

    def row_term(s, carry):
        base = (s * ROWS).astype(jnp.float32)
        hit = wide(own_part[...]) == lane_f + base
        coef = p_all[s] * meta[s, 1:2, :] * wide(tot_s[...]) - jnp.where(hit, 1.0, 0.0)
        g_s[...] += nn(coef.astype(jnp.bfloat16), e_all[s])
        return carry

    lax.fori_loop(0, 16, row_term, 0)

    for k in range(1, 16):
        slot = (pool + k) % 16
        pltpu.make_async_remote_copy(
            src_ref=recips.at[slot], dst_ref=recips.at[slot],
            send_sem=r_ssem.at[0], recv_sem=r_rsem.at[slot],
            device_id=(dp, pool), device_id_type=MESH,
        ).wait_recv()

    mine = (pool * ROWS).astype(jnp.float32)

    def col_term(s, carry):
        hit = meta[s, 0:1, :] == row_f + mine
        coef = p_all[s] * wide(own_w[...]) * recips[s] - jnp.where(hit, 1.0, 0.0)
        g_s[...] += nn(coef.astype(jnp.bfloat16), e_all[s])
        return carry

    lax.fori_loop(0, 16, col_term, 0)

    g = g_s[...]
    nrm = normed_s[...]
    g = (g - nrm * jnp.sum(nrm * g, axis=1, keepdims=True)) * wide(inv_s[...])
    gp = g.astype(jnp.bfloat16)

    a_own = y * (1 - core) + x * core
    b_own = x * (1 - core) + y * core
    for t in (2, 1, 3, 0):
        a = (b_own + t) % 4
        core_send[a] = nn(feats_t[1, pl.ds(pl.multiple_of(a * 256, 256), 256), :], gp).astype(core_send.dtype)
        c = pltpu.make_async_remote_copy(
            src_ref=core_send.at[a], dst_ref=core_recv.at[a],
            send_sem=c_ssem.at[a], recv_sem=c_rsem.at[a],
            device_id=(y * 4 + zh * 2 + (1 - core), pool), device_id_type=MESH,
        )
        c.start()
        pending.append(c)
    for t in (2, 1, 3, 0):
        a = (a_own + t) % 4
        own = nn(feats_t[0, pl.ds(pl.multiple_of(a * 256, 256), 256), :], gp)
        pltpu.make_async_remote_copy(
            src_ref=core_send.at[a], dst_ref=core_recv.at[a],
            send_sem=c_ssem.at[a], recv_sem=c_rsem.at[a],
            device_id=(dp, pool), device_id_type=MESH,
        ).wait_recv()
        own = own + core_recv[a].astype(jnp.float32)
        if t:
            send2[a] = own.astype(send2.dtype)
            ty = a * (1 - core) + y * core
            tx = x * (1 - core) + a * core
            c = pltpu.make_async_remote_copy(
                src_ref=send2.at[a], dst_ref=recv2.at[a_own],
                send_sem=s2_sem.at[a], recv_sem=r2_sem.at[a_own],
                device_id=(ty * 4 + zh * 2 + core, tx * 4 + z), device_id_type=MESH,
            )
            c.start()
            pending.append(c)
        else:
            for q in range(4):
                acc2[q] = own[q * 64:(q + 1) * 64]
    for t in (1, 3, 2):
        a = (a_own + t) % 4
        pltpu.make_async_remote_copy(
            src_ref=send2.at[a], dst_ref=recv2.at[a],
            send_sem=s2_sem.at[a], recv_sem=r2_sem.at[a],
            device_id=(dp, pool), device_id_type=MESH,
        ).wait_recv()
    for t in (2, 1, 3, 0):
        b = (b_own + t) % 4
        part = acc2[b]
        rows = pl.ds(pl.multiple_of(b * 64, 64), 64)
        for u in (1, 2, 3):
            part = part + recv2[(a_own + u) % 4, rows, :].astype(jnp.float32)
        send3[b] = part.astype(send3.dtype)
        if t:
            ty = y * (1 - core) + b * core
            tx = b * (1 - core) + x * core
            c = pltpu.make_async_remote_copy(
                src_ref=send3.at[b], dst_ref=recv3.at[b_own],
                send_sem=s3_sem.at[b], recv_sem=r3_sem.at[b_own],
                device_id=(ty * 4 + zh * 2 + core, tx * 4 + z), device_id_type=MESH,
            )
            c.start()
            pending.append(c)
    part = send3[b_own]
    for t in (1, 3, 2):
        b = (b_own + t) % 4
        pltpu.make_async_remote_copy(
            src_ref=send3.at[b], dst_ref=recv3.at[b],
            send_sem=s3_sem.at[b], recv_sem=r3_sem.at[b],
            device_id=(dp, pool), device_id_type=MESH,
        ).wait_recv()
        part = part + recv3[b]
    for q in range(8):
        send4[q] = part[q * 8:(q + 1) * 8]
    zz = zh * 4 + z
    for t in (4, 3, 5, 2, 6, 1, 7):
        q = (zz + t) % 8
        c = pltpu.make_async_remote_copy(
            src_ref=send4.at[q], dst_ref=recv4.at[zz],
            send_sem=s4_sem.at[q], recv_sem=r4_sem.at[zz],
            device_id=(y * 4 + (q // 4) * 2 + core, x * 4 + q % 4), device_id_type=MESH,
        )
        c.start()
        pending.append(c)
    result = send4[zz]
    for t in (1, 7, 2, 6, 3, 5, 4):
        q = (zz + t) % 8
        pltpu.make_async_remote_copy(
            src_ref=send4.at[q], dst_ref=recv4.at[q],
            send_sem=s4_sem.at[q], recv_sem=r4_sem.at[q],
            device_id=(dp, pool), device_id_type=MESH,
        ).wait_recv()
        result = result + recv4[q]
    out_ref[...] = result
    for c in pending:
        c.wait_send()


def per_device(feats, tower_w, partners, popularity_buckets, row_counts):
    f32, bf16 = jnp.float32, jnp.bfloat16
    vmem = pltpu.VMEM
    dma = pltpu.SemaphoreType.DMA
    return pl.pallas_call(
        kernel,
        out_shape=jax.ShapeDtypeStruct((8, DE), f32),
        in_specs=[
            pl.BlockSpec(memory_space=pl.ANY),
            pl.BlockSpec(memory_space=pl.ANY),
            pl.BlockSpec(memory_space=pltpu.VMEM),
            pl.BlockSpec(memory_space=pltpu.VMEM),
            pl.BlockSpec(memory_space=pltpu.SMEM),
        ],
        out_specs=pl.BlockSpec(memory_space=pltpu.VMEM),
        scratch_shapes=[
            vmem((ROWS, DIN), bf16),
            vmem((DIN, DE), bf16),
            vmem((2, 1024, ROWS), bf16),
            vmem((16, ROWS, DE), bf16),
            vmem((16, ROWS, ROWS), f32),
            vmem((16, 2, ROWS), f32),
            vmem((16, 1, ROWS), f32),
            vmem((ROWS, DE), f32),
            vmem((ROWS, 128), f32),
            vmem((ROWS, 128), f32),
            vmem((ROWS, 128), f32),
            vmem((ROWS, 128), f32),
            vmem((ROWS, 128), f32),
            vmem((ROWS, DE), f32),
            vmem((4, 256, DE), bf16),
            vmem((4, 256, DE), bf16),
            vmem((4, 256, DE), bf16),
            vmem((4, 256, DE), bf16),
            vmem((4, 64, DE), f32),
            vmem((4, 64, DE), f32),
            vmem((4, 64, DE), f32),
            vmem((8, 8, DE), f32),
            vmem((8, 8, DE), f32),
            dma((KC, 2)),
            dma((16,)),
            dma((16,)),
            dma((32,)),
            dma((16, 2)),
            dma((16,)),
            dma((16,)),
            dma((4,)),
            dma((4,)),
            dma((4,)),
            dma((4,)),
            dma((4,)),
            dma((4,)),
            dma((8,)),
            dma((8,)),
        ],
        compiler_params=pltpu.CompilerParams(collective_id=0, has_side_effects=True),
    )(feats, tower_w, partners.reshape(1, ROWS), popularity_buckets.reshape(1, ROWS), row_counts)


def solution(mesh):
    return jax.shard_map(
        per_device,
        mesh=mesh,
        in_specs=(P(("dp", "pool"), None), P(), P(("dp", "pool")), P(("dp", "pool")), P()),
        out_specs=P(("dp", "pool"), None),
        check_vma=False,
    )
```

```python
import functools

import jax
import jax.numpy as jnp
from jax import lax
from jax.experimental import pallas as pl
from jax.experimental.pallas import tpu as pltpu
from jax.sharding import PartitionSpec as P

MESH = pl.DeviceIdType.MESH
EPS = 1e-06
SCALE = 28.853900817779268
ROWS = 256
HALF = 128
DE = 256
DIN = 2048
KC = 4
KW = DIN // KC


def nt(left, right):
    return lax.dot_general(
        left, right, (((1,), (1,)), ((), ())), preferred_element_type=jnp.float32
    )


def nn(left, right):
    return jnp.dot(left, right, preferred_element_type=jnp.float32)


def kernel(
    feats_hbm, w_hbm, part_hbm, buck_hbm, counts_hbm, out_ref,
    feats_v, w_v, part_v, buck_v, counts_v, feats_t, e_all, a_all, b_all, meta, recips,
    normed_s, inv_s, own_w, own_part, own_valid, tot_s, g_s,
    core_send, core_recv, keep2, send2, recv2, send3, recv3, send4, recv4,
    in_sem, small_sem, meta_ssem, meta_rsem, e_ssem, e_rsem, r_ssem, r_rsem,
    c_ssem, c_rsem, s2_sem, r2_sem, s3_sem, r3_sem, s4_sem, r4_sem,
):
    dp = lax.axis_index("dp")
    pool = lax.axis_index("pool")
    y = dp // 4
    zh = (dp // 2) % 2
    core = dp % 2
    x = pool // 4
    z = pool % 4
    zs = [z, z + 1 - 2 * (z % 2), (z + 2) % 4, 3 - z]

    barrier = pltpu.get_barrier_semaphore()

    def greet(d, p):
        pl.semaphore_signal(barrier, inc=1, device_id=(d, p), device_id_type=MESH)

    for k in range(1, 16):
        greet(dp, (pool + k) % 16)
    greet(y * 4 + zh * 2 + (1 - core), pool)
    for k in range(1, 4):
        greet(((y + k) % 4) * 4 + zh * 2 + core, pool)
    for k in range(4):
        greet(y * 4 + (1 - zh) * 2 + core, x * 4 + k)

    loads = []
    for k in range(KC):
        cols = pl.ds(k * KW, KW)
        a = pltpu.make_async_copy(feats_hbm.at[:, cols], feats_v.at[:, cols], in_sem.at[k, 0])
        b = pltpu.make_async_copy(w_hbm.at[cols, :], w_v.at[cols, :], in_sem.at[k, 1])
        a.start()
        b.start()
        loads.append((a, b))
    small = [
        pltpu.make_async_copy(part_hbm, part_v, small_sem.at[0]),
        pltpu.make_async_copy(buck_hbm, buck_v, small_sem.at[1]),
        pltpu.make_async_copy(counts_hbm, counts_v, small_sem.at[2]),
    ]
    for c in small:
        c.start()

    projected = None
    for k in range(KC):
        loads[k][0].wait()
        loads[k][1].wait()
        cols = pl.ds(k * KW, KW)
        term = nn(feats_v[:, cols], w_v[cols, :])
        projected = term if projected is None else projected + term
    inv_norm = lax.rsqrt(jnp.sum(projected * projected, axis=1, keepdims=True) + EPS)
    normed = projected * inv_norm
    normed_s[...] = normed
    inv_s[...] = jnp.broadcast_to(inv_norm, (ROWS, 128))
    e_all[pool] = normed.astype(jnp.bfloat16)

    for c in small:
        c.wait()
    cnt = counts_v[dp, pool]
    lane = lax.broadcasted_iota(jnp.int32, (1, ROWS), 1)
    valid = lane < cnt
    part_l = jnp.where(valid, part_v[...], -1).astype(jnp.float32)
    w_l = jnp.where(valid, jnp.exp((buck_v[...].astype(jnp.float32) + 0.5) * 0.25), 0.0)
    meta[pool, 0:1, :] = part_l
    meta[pool, 1:2, :] = w_l

    pl.semaphore_wait(barrier, 23)

    pending = []

    def rows_of(h):
        return pl.ds(h * HALF, HALF)

    def send(slot, h, target, n):
        c = pltpu.make_async_remote_copy(
            src_ref=e_all.at[slot, rows_of(h)], dst_ref=e_all.at[slot, rows_of(h)],
            send_sem=e_ssem.at[n], recv_sem=e_rsem.at[slot, h],
            device_id=(dp, target), device_id_type=MESH,
        )
        c.start()
        pending.append(c)

    def arrive(slot, h):
        pltpu.make_async_remote_copy(
            src_ref=e_all.at[slot, rows_of(h)], dst_ref=e_all.at[slot, rows_of(h)],
            send_sem=e_ssem.at[0], recv_sem=e_rsem.at[slot, h],
            device_id=(dp, pool), device_id_type=MESH,
        ).wait_recv()

    def meta_arrive(slot):
        pltpu.make_async_remote_copy(
            src_ref=meta.at[slot], dst_ref=meta.at[slot],
            send_sem=meta_ssem.at[0], recv_sem=meta_rsem.at[slot],
            device_id=(dp, pool), device_id_type=MESH,
        ).wait_recv()

    right = (x + 1) % 4
    left = (x + 3) % 4
    far = (x + 2) % 4
    count = iter(range(64))
    for h in (0, 1):
        send(pool, h, right * 4 + z, next(count))
        send(pool, 1 - h, left * 4 + z, next(count))
    for c in (1, 2, 3):
        for h in (0, 1):
            send(pool, h, x * 4 + zs[c], next(count))
    for k in range(1, 16):
        c = pltpu.make_async_remote_copy(
            src_ref=meta.at[pool], dst_ref=meta.at[pool],
            send_sem=meta_ssem.at[k], recv_sem=meta_rsem.at[pool],
            device_id=(dp, (pool + k) % 16), device_id_type=MESH,
        )
        c.start()
        pending.append(c)

    own_part[...] = jnp.broadcast_to(part_l, (128, ROWS)).T
    own_w[...] = jnp.broadcast_to(w_l, (128, ROWS)).T
    own_valid[...] = jnp.broadcast_to(jnp.where(valid, 1.0, 0.0), (128, ROWS)).T

    def wide(v):
        return jnp.concatenate([v, v], axis=1)

    def scores(slot, first=False):
        s = nt(e_all[pool], e_all[slot])
        e = jnp.exp2(s * SCALE)
        if first:
            ri = lax.broadcasted_iota(jnp.int32, (ROWS, ROWS), 0)
            ci = lax.broadcasted_iota(jnp.int32, (ROWS, ROWS), 1)
            e = jnp.where(ri == ci, 0.0, e)
        b_all[slot] = e * wide(own_w[...])
        t = e * meta[slot, 1:2, :]
        a_all[slot] = t
        t = t[:, :128] + t[:, 128:]
        if first:
            tot_s[...] = t
        else:
            tot_s[...] += t

    scores(pool, True)

    def transposes(lo, hi):
        for m in range(lo, hi):
            my, mz, mc = m // 4, (m // 2) % 2, m % 2
            t = feats_v[:, m * 128:(m + 1) * 128].T
            which = (mc + core) % 2
            for mx in range(4):
                at = (my * (2 + 6 * mc) + mx * (8 - 6 * mc) + mz) * 32
                feats_t[which, at:at + 32, :] = t[mx * 32:(mx + 1) * 32]

    transposes(0, 8)

    for c in range(4):
        if c < 3:
            nslot = x * 4 + zs[c + 1]
            for h in (0, 1):
                arrive(nslot, h)
                send(nslot, h, right * 4 + z, next(count))
                send(nslot, h, left * 4 + z, next(count))
        ls = left * 4 + zs[c]
        rs = right * 4 + zs[c]
        arrive(ls, 0)
        send(ls, 0, right * 4 + z, next(count))
        arrive(rs, 1)
        send(rs, 1, left * 4 + z, next(count))
        if c == 0:
            transposes(8, 16)
        if c < 3:
            meta_arrive(nslot)
            scores(nslot)
        arrive(ls, 1)
        meta_arrive(ls)
        scores(ls)
        arrive(rs, 0)
        meta_arrive(rs)
        scores(rs)
        if c > 0:
            fs = far * 4 + zs[c - 1]
            arrive(fs, 0)
            arrive(fs, 1)
            meta_arrive(fs)
            scores(fs)
    fs = far * 4 + zs[3]
    arrive(fs, 0)
    arrive(fs, 1)
    meta_arrive(fs)
    scores(fs)

    order = [
        [(2, 3), (2, 2), (2, 1), (3, 3)],
        [(1, 3), (3, 2), (1, 2), (2, 0)],
        [(3, 1), (1, 1), (0, 3), (0, 2)],
        [(3, 0), (1, 0), (0, 1), (0, 0)],
    ]

    def member(dx, c):
        return ((x + dx) % 4) * 4 + zs[c]

    total = jnp.broadcast_to(jnp.sum(tot_s[...], axis=1, keepdims=True), (ROWS, 128))
    recip_own = own_valid[...] / total
    recips[pool] = recip_own.T[0:1, :]
    n = 0
    for group in order:
        for dx, c in group:
            if (dx, c) == (0, 0):
                continue
            cp = pltpu.make_async_remote_copy(
                src_ref=recips.at[pool], dst_ref=recips.at[pool],
                send_sem=r_ssem.at[n], recv_sem=r_rsem.at[pool],
                device_id=(dp, member(dx, c)), device_id_type=MESH,
            )
            cp.start()
            pending.append(cp)
            n += 1

    tot_s[...] = recip_own
    g_s[...] = jnp.zeros_like(g_s)
    lane_f = lax.broadcasted_iota(jnp.int32, (1, ROWS), 1).astype(jnp.float32)

    def row_term(i, carry):
        acc = None
        for j in range(4):
            s = i * 4 + j
            hit = wide(own_part[...]) == lane_f + (s * ROWS).astype(jnp.float32)
            coef = a_all[s] * wide(tot_s[...])
            coef = jnp.where(hit, coef - 1.0, coef).astype(jnp.bfloat16)
            term = nn(coef, e_all[s])
            acc = term if acc is None else acc + term
        g_s[...] += acc
        return carry

    lax.fori_loop(0, 4, row_term, 0)

    mine = lax.broadcasted_iota(jnp.int32, (ROWS, 128), 0).astype(jnp.float32) + (pool * ROWS).astype(jnp.float32)
    own_part[...] = mine
    for group in order[::-1]:
        slots = [member(dx, c) for dx, c in group[::-1]]
        for (dx, c), s in zip(group[::-1], slots):
            if (dx, c) == (0, 0):
                continue
            pltpu.make_async_remote_copy(
                src_ref=recips.at[s], dst_ref=recips.at[s],
                send_sem=r_ssem.at[0], recv_sem=r_rsem.at[s],
                device_id=(dp, pool), device_id_type=MESH,
            ).wait_recv()
        acc = None
        for s in slots:
            hit = wide(own_part[...]) == meta[s, 0:1, :]
            coef = b_all[s] * recips[s]
            coef = jnp.where(hit, coef - 1.0, coef).astype(jnp.bfloat16)
            term = nn(coef, e_all[s])
            acc = term if acc is None else acc + term
        g_s[...] += acc

    g = g_s[...]
    nrm = normed_s[...]
    g = (g - nrm * jnp.sum(nrm * g, axis=1, keepdims=True)) * wide(inv_s[...])
    gp = g.astype(jnp.bfloat16)

    a_own = y * (1 - core) + x * core
    b_own = x * (1 - core) + y * core
    turns = (2, 1, 3, 0)
    for t in turns:
        b = (a_own + t) % 4
        core_send[b] = nn(feats_t[1, pl.ds(pl.multiple_of(b * 256, 256), 256), :], gp).astype(core_send.dtype)
        c = pltpu.make_async_remote_copy(
            src_ref=core_send.at[b], dst_ref=core_recv.at[b],
            send_sem=c_ssem.at[b], recv_sem=c_rsem.at[b],
            device_id=(y * 4 + zh * 2 + (1 - core), pool), device_id_type=MESH,
        )
        c.start()
        pending.append(c)
    for t in turns:
        b = (b_own + t) % 4
        own = nn(feats_t[0, pl.ds(pl.multiple_of(b * 256, 256), 256), :], gp)
        pltpu.make_async_remote_copy(
            src_ref=core_send.at[b], dst_ref=core_recv.at[b],
            send_sem=c_ssem.at[b], recv_sem=c_rsem.at[b],
            device_id=(dp, pool), device_id_type=MESH,
        ).wait_recv()
        own = own + core_recv[b].astype(jnp.float32)
        for q in range(4):
            keep2[b, q] = own[q * 64:(q + 1) * 64]
            send2[b, q] = own[q * 64:(q + 1) * 64].astype(send2.dtype)
        for u in (2, 1, 3):
            a = (a_own + u) % 4
            ty = a * (1 - core) + y * core
            tx = x * (1 - core) + a * core
            c = pltpu.make_async_remote_copy(
                src_ref=send2.at[b, a], dst_ref=recv2.at[b, a_own],
                send_sem=s2_sem.at[b, a], recv_sem=r2_sem.at[b, a_own],
                device_id=(ty * 4 + zh * 2 + core, tx * 4 + z), device_id_type=MESH,
            )
            c.start()
            pending.append(c)
    for t in turns:
        b = (b_own + t) % 4
        part = keep2[b, a_own]
        for u in (1, 3, 2):
            a = (a_own + u) % 4
            pltpu.make_async_remote_copy(
                src_ref=send2.at[b, a], dst_ref=recv2.at[b, a],
                send_sem=s2_sem.at[b, a], recv_sem=r2_sem.at[b, a],
                device_id=(dp, pool), device_id_type=MESH,
            ).wait_recv()
            part = part + recv2[b, a].astype(jnp.float32)
        if t:
            send3[b] = part.astype(send3.dtype)
            ty = y * (1 - core) + b * core
            tx = b * (1 - core) + x * core
            c = pltpu.make_async_remote_copy(
                src_ref=send3.at[b], dst_ref=recv3.at[b_own],
                send_sem=s3_sem.at[b], recv_sem=r3_sem.at[b_own],
                device_id=(ty * 4 + zh * 2 + core, tx * 4 + z), device_id_type=MESH,
            )
            c.start()
            pending.append(c)
    for t in (1, 3, 2):
        b = (b_own + t) % 4
        pltpu.make_async_remote_copy(
            src_ref=send3.at[b], dst_ref=recv3.at[b],
            send_sem=s3_sem.at[b], recv_sem=r3_sem.at[b],
            device_id=(dp, pool), device_id_type=MESH,
        ).wait_recv()
        part = part + recv3[b].astype(jnp.float32)
    for q in range(8):
        send4[q] = part[q * 8:(q + 1) * 8]
    zz = zh * 4 + z
    for t in (4, 3, 5, 2, 6, 1, 7):
        q = (zz + t) % 8
        c = pltpu.make_async_remote_copy(
            src_ref=send4.at[q], dst_ref=recv4.at[zz],
            send_sem=s4_sem.at[q], recv_sem=r4_sem.at[zz],
            device_id=(y * 4 + (q // 4) * 2 + core, x * 4 + q % 4), device_id_type=MESH,
        )
        c.start()
        pending.append(c)
    result = send4[zz]
    for t in (1, 7, 2, 6, 3, 5, 4):
        q = (zz + t) % 8
        pltpu.make_async_remote_copy(
            src_ref=send4.at[q], dst_ref=recv4.at[q],
            send_sem=s4_sem.at[q], recv_sem=r4_sem.at[q],
            device_id=(dp, pool), device_id_type=MESH,
        ).wait_recv()
        result = result + recv4[q]
    out_ref[...] = result
    for c in pending:
        c.wait_send()


def per_device(feats, tower_w, partners, popularity_buckets, row_counts):
    f32, bf16, i32 = jnp.float32, jnp.bfloat16, jnp.int32
    vmem = pltpu.VMEM
    dma = pltpu.SemaphoreType.DMA
    return pl.pallas_call(
        kernel,
        out_shape=pltpu.VMEM((8, DE), f32),
        in_specs=[pl.BlockSpec(memory_space=pl.ANY)] * 5,
        out_specs=pl.BlockSpec(memory_space=pltpu.VMEM),
        scratch_shapes=[
            vmem((ROWS, DIN), bf16),
            vmem((DIN, DE), bf16),
            vmem((1, ROWS), i32),
            vmem((1, ROWS), i32),
            pltpu.SMEM((16, 16), i32),
            vmem((2, 1024, ROWS), bf16),
            vmem((16, ROWS, DE), bf16),
            vmem((16, ROWS, ROWS), f32),
            vmem((16, ROWS, ROWS), f32),
            vmem((16, 2, ROWS), f32),
            vmem((16, 1, ROWS), f32),
            vmem((ROWS, DE), f32),
            vmem((ROWS, 128), f32),
            vmem((ROWS, 128), f32),
            vmem((ROWS, 128), f32),
            vmem((ROWS, 128), f32),
            vmem((ROWS, 128), f32),
            vmem((ROWS, DE), f32),
            vmem((4, 256, DE), bf16),
            vmem((4, 256, DE), bf16),
            vmem((4, 4, 64, DE), f32),
            vmem((4, 4, 64, DE), bf16),
            vmem((4, 4, 64, DE), bf16),
            vmem((4, 64, DE), f32),
            vmem((4, 64, DE), f32),
            vmem((8, 8, DE), f32),
            vmem((8, 8, DE), f32),
            dma((KC, 2)),
            dma((3,)),
            dma((16,)),
            dma((16,)),
            dma((32,)),
            dma((16, 2)),
            dma((16,)),
            dma((16,)),
            dma((4,)),
            dma((4,)),
            dma((4, 4)),
            dma((4, 4)),
            dma((4,)),
            dma((4,)),
            dma((8,)),
            dma((8,)),
        ],
        compiler_params=pltpu.CompilerParams(collective_id=0, has_side_effects=True),
    )(feats, tower_w, partners.reshape(1, ROWS), popularity_buckets.reshape(1, ROWS), row_counts)


def solution(mesh):
    return jax.shard_map(
        per_device,
        mesh=mesh,
        in_specs=(P(("dp", "pool"), None), P(), P(("dp", "pool")), P(("dp", "pool")), P()),
        out_specs=P(("dp", "pool"), None),
        check_vma=False,
    )
```

```python
import functools

import jax
import jax.numpy as jnp
from jax import lax
from jax.experimental import pallas as pl
from jax.experimental.pallas import tpu as pltpu
from jax.sharding import PartitionSpec as P

MESH = pl.DeviceIdType.MESH
EPS = 1e-06
SCALE = 28.853900817779268
ROWS = 256
HALF = 128
DE = 256
DIN = 2048
KC = 4
KW = DIN // KC


def nt(left, right):
    return lax.dot_general(
        left, right, (((1,), (1,)), ((), ())), preferred_element_type=jnp.float32
    )


def nn(left, right):
    return jnp.dot(left, right, preferred_element_type=jnp.float32)


def kernel(
    feats_hbm, w_hbm, part_hbm, buck_hbm, counts_hbm, out_ref,
    feats_v, w_v, part_v, buck_v, counts_v, feats_t, e_all, a_all, b_all, meta, recips,
    normed_s, inv_s, own_w, own_part, own_valid, tot_s, g_s,
    core_send, core_recv, keep2, send2, recv2, send3, recv3, send4, recv4,
    in_sem, small_sem, meta_ssem, meta_rsem, e_ssem, e_rsem, r_ssem, r_rsem,
    c_ssem, c_rsem, s2_sem, r2_sem, s3_sem, r3_sem, s4_sem, r4_sem,
):
    dp = lax.axis_index("dp")
    pool = lax.axis_index("pool")
    y = dp // 4
    zh = (dp // 2) % 2
    core = dp % 2
    x = pool // 4
    z = pool % 4
    zs = [z, z + 1 - 2 * (z % 2), (z + 2) % 4, 3 - z]

    barrier = pltpu.get_barrier_semaphore()

    def greet(d, p):
        pl.semaphore_signal(barrier, inc=1, device_id=(d, p), device_id_type=MESH)

    for k in range(1, 16):
        greet(dp, (pool + k) % 16)
    greet(y * 4 + zh * 2 + (1 - core), pool)
    for k in range(1, 4):
        greet(((y + k) % 4) * 4 + zh * 2 + core, pool)
    for k in range(4):
        greet(y * 4 + (1 - zh) * 2 + core, x * 4 + k)

    loads = []
    for k in range(KC):
        cols = pl.ds(k * KW, KW)
        a = pltpu.make_async_copy(feats_hbm.at[:, cols], feats_v.at[:, cols], in_sem.at[k, 0])
        b = pltpu.make_async_copy(w_hbm.at[cols, :], w_v.at[cols, :], in_sem.at[k, 1])
        a.start()
        b.start()
        loads.append((a, b))
    small = [
        pltpu.make_async_copy(part_hbm, part_v, small_sem.at[0]),
        pltpu.make_async_copy(buck_hbm, buck_v, small_sem.at[1]),
        pltpu.make_async_copy(counts_hbm, counts_v, small_sem.at[2]),
    ]
    for c in small:
        c.start()

    projected = None
    for k in range(KC):
        loads[k][0].wait()
        loads[k][1].wait()
        cols = pl.ds(k * KW, KW)
        term = nn(feats_v[:, cols], w_v[cols, :])
        projected = term if projected is None else projected + term
    inv_norm = lax.rsqrt(jnp.sum(projected * projected, axis=1, keepdims=True) + EPS)
    normed = projected * inv_norm
    normed_s[...] = normed
    inv_s[...] = jnp.broadcast_to(inv_norm, (ROWS, 128))
    e_all[pool] = normed.astype(jnp.bfloat16)

    for c in small:
        c.wait()
    cnt = counts_v[dp, pool]
    lane = lax.broadcasted_iota(jnp.int32, (1, ROWS), 1)
    valid = lane < cnt
    part_l = jnp.where(valid, part_v[...], -1).astype(jnp.float32)
    w_l = jnp.where(valid, jnp.exp((buck_v[...].astype(jnp.float32) + 0.5) * 0.25), 0.0)
    meta[pool, 0:1, :] = part_l
    meta[pool, 1:2, :] = w_l

    pl.semaphore_wait(barrier, 23)

    pending = []

    def rows_of(h):
        return pl.ds(h * HALF, HALF)

    def send(slot, h, target, n):
        c = pltpu.make_async_remote_copy(
            src_ref=e_all.at[slot, rows_of(h)], dst_ref=e_all.at[slot, rows_of(h)],
            send_sem=e_ssem.at[n], recv_sem=e_rsem.at[slot, h],
            device_id=(dp, target), device_id_type=MESH,
        )
        c.start()
        pending.append(c)

    def arrive(slot, h):
        pltpu.make_async_remote_copy(
            src_ref=e_all.at[slot, rows_of(h)], dst_ref=e_all.at[slot, rows_of(h)],
            send_sem=e_ssem.at[0], recv_sem=e_rsem.at[slot, h],
            device_id=(dp, pool), device_id_type=MESH,
        ).wait_recv()

    def meta_arrive(slot):
        pltpu.make_async_remote_copy(
            src_ref=meta.at[slot], dst_ref=meta.at[slot],
            send_sem=meta_ssem.at[0], recv_sem=meta_rsem.at[slot],
            device_id=(dp, pool), device_id_type=MESH,
        ).wait_recv()

    right = (x + 1) % 4
    left = (x + 3) % 4
    far = (x + 2) % 4
    middle = z % 2 + z // 2 == 1
    count = iter(range(64))
    inner = []

    def to_right(slot, h):
        send(slot, h, right * 4 + z, next(count))

    def to_left(slot, h):
        send(slot, h, left * 4 + z, next(count))

    def to_z(slot, h, c):
        send(slot, h, x * 4 + zs[c], next(count))

    def to_z_from_middle(slot, h, c):
        n = next(count)
        cp = pltpu.make_async_remote_copy(
            src_ref=e_all.at[slot, rows_of(h)], dst_ref=e_all.at[slot, rows_of(h)],
            send_sem=e_ssem.at[n], recv_sem=e_rsem.at[slot, h],
            device_id=(dp, x * 4 + zs[c]), device_id_type=MESH,
        )
        inner.append(cp)
        pl.when(middle)(cp.start)

    for h in (0, 1):
        to_right(pool, h)
        to_left(pool, 1 - h)
        to_z(pool, h, 1)
    for h in (0, 1):
        to_z(pool, h, 2)
    for h in (0, 1):
        to_z_from_middle(pool, h, 3)
    for k in range(1, 16):
        c = pltpu.make_async_remote_copy(
            src_ref=meta.at[pool], dst_ref=meta.at[pool],
            send_sem=meta_ssem.at[k], recv_sem=meta_rsem.at[pool],
            device_id=(dp, (pool + k) % 16), device_id_type=MESH,
        )
        c.start()
        pending.append(c)

    own_part[...] = jnp.broadcast_to(part_l, (128, ROWS)).T
    own_w[...] = jnp.broadcast_to(w_l, (128, ROWS)).T
    own_valid[...] = jnp.broadcast_to(jnp.where(valid, 1.0, 0.0), (128, ROWS)).T

    def wide(v):
        return jnp.concatenate([v, v], axis=1)

    def scores(slot, first=False):
        s = nt(e_all[pool], e_all[slot])
        e = jnp.exp2(s * SCALE)
        if first:
            ri = lax.broadcasted_iota(jnp.int32, (ROWS, ROWS), 0)
            ci = lax.broadcasted_iota(jnp.int32, (ROWS, ROWS), 1)
            e = jnp.where(ri == ci, 0.0, e)
        b_all[slot] = e * wide(own_w[...])
        t = e * meta[slot, 1:2, :]
        a_all[slot] = t
        t = t[:, :128] + t[:, 128:]
        if first:
            tot_s[...] = t
        else:
            tot_s[...] += t

    scores(pool, True)

    def transposes(lo, hi):
        for m in range(lo, hi):
            my, mz, mc = m // 4, (m // 2) % 2, m % 2
            t = feats_v[:, m * 128:(m + 1) * 128].T
            which = (mc + core) % 2
            for mx in range(4):
                at = (my * (2 + 6 * mc) + mx * (8 - 6 * mc) + mz) * 32
                feats_t[which, at:at + 32, :] = t[mx * 32:(mx + 1) * 32]

    transposes(0, 8)

    def member(dx, c):
        return ((x + dx) % 4) * 4 + zs[c]

    def take(slot):
        meta_arrive(slot)
        scores(slot)

    def turn(c):
        arrive(member(3, c), 0)
        to_right(member(3, c), 0)
        arrive(member(1, c), 1)
        to_left(member(1, c), 1)

    def spread(c):
        for h in (0, 1):
            arrive(member(0, c), h)
            to_right(member(0, c), h)
            to_left(member(0, c), h)
            if c == 2:
                to_z_from_middle(member(0, c), h, 1)

    def rest(c):
        arrive(member(3, c), 1)
        take(member(3, c))
        arrive(member(1, c), 0)
        take(member(1, c))

    turn(0)
    spread(1)
    transposes(8, 16)
    take(member(0, 1))
    rest(0)
    for h in (0, 1):
        arrive(member(2, 0), h)
        to_z(member(2, 0), h, 1)
        to_z(member(2, 0), h, 3)
    take(member(2, 0))
    spread(2)
    take(member(0, 2))
    for h in (0, 1):
        arrive(member(3, 1), h)
        arrive(member(1, 1), h)
    take(member(3, 1))
    take(member(1, 1))
    turn(2)
    spread(3)
    take(member(0, 3))
    rest(2)
    arrive(member(2, 1), 0)
    arrive(member(2, 1), 1)
    take(member(2, 1))
    arrive(member(2, 2), 0)
    arrive(member(2, 2), 1)
    take(member(2, 2))
    arrive(member(2, 3), 0)
    arrive(member(2, 3), 1)
    take(member(2, 3))
    for h in (0, 1):
        arrive(member(3, 3), h)
        arrive(member(1, 3), h)
    take(member(3, 3))
    take(member(1, 3))

    order = [
        [(2, 3), (2, 2), (2, 1), (3, 3)],
        [(1, 3), (3, 2), (1, 2), (2, 0)],
        [(3, 1), (1, 1), (0, 3), (0, 2)],
        [(3, 0), (1, 0), (0, 1), (0, 0)],
    ]

    total = jnp.broadcast_to(jnp.sum(tot_s[...], axis=1, keepdims=True), (ROWS, 128))
    recip_own = own_valid[...] / total
    recips[pool] = recip_own.T[0:1, :]
    n = 0
    for group in order:
        for dx, c in group:
            if (dx, c) == (0, 0):
                continue
            cp = pltpu.make_async_remote_copy(
                src_ref=recips.at[pool], dst_ref=recips.at[pool],
                send_sem=r_ssem.at[n], recv_sem=r_rsem.at[pool],
                device_id=(dp, member(dx, c)), device_id_type=MESH,
            )
            cp.start()
            pending.append(cp)
            n += 1

    tot_s[...] = recip_own
    g_s[...] = jnp.zeros_like(g_s)
    lane_f = lax.broadcasted_iota(jnp.int32, (1, ROWS), 1).astype(jnp.float32)

    def row_term(i, carry):
        acc = None
        for j in range(4):
            s = i * 4 + j
            hit = wide(own_part[...]) == lane_f + (s * ROWS).astype(jnp.float32)
            coef = a_all[s] * wide(tot_s[...])
            coef = jnp.where(hit, coef - 1.0, coef).astype(jnp.bfloat16)
            term = nn(coef, e_all[s])
            acc = term if acc is None else acc + term
        g_s[...] += acc
        return carry

    lax.fori_loop(0, 4, row_term, 0)

    mine = lax.broadcasted_iota(jnp.int32, (ROWS, 128), 0).astype(jnp.float32) + (pool * ROWS).astype(jnp.float32)
    own_part[...] = mine
    for group in order[::-1]:
        slots = [member(dx, c) for dx, c in group[::-1]]
        for (dx, c), s in zip(group[::-1], slots):
            if (dx, c) == (0, 0):
                continue
            pltpu.make_async_remote_copy(
                src_ref=recips.at[s], dst_ref=recips.at[s],
                send_sem=r_ssem.at[0], recv_sem=r_rsem.at[s],
                device_id=(dp, pool), device_id_type=MESH,
            ).wait_recv()
        acc = None
        for s in slots:
            hit = wide(own_part[...]) == meta[s, 0:1, :]
            coef = b_all[s] * recips[s]
            coef = jnp.where(hit, coef - 1.0, coef).astype(jnp.bfloat16)
            term = nn(coef, e_all[s])
            acc = term if acc is None else acc + term
        g_s[...] += acc

    g = g_s[...]
    nrm = normed_s[...]
    g = (g - nrm * jnp.sum(nrm * g, axis=1, keepdims=True)) * wide(inv_s[...])
    gp = g.astype(jnp.bfloat16)

    a_own = y * (1 - core) + x * core
    b_own = x * (1 - core) + y * core
    turns = (2, 1, 3, 0)
    for t in turns:
        b = (a_own + t) % 4
        core_send[b] = nn(feats_t[1, pl.ds(pl.multiple_of(b * 256, 256), 256), :], gp).astype(core_send.dtype)
        c = pltpu.make_async_remote_copy(
            src_ref=core_send.at[b], dst_ref=core_recv.at[b],
            send_sem=c_ssem.at[b], recv_sem=c_rsem.at[b],
            device_id=(y * 4 + zh * 2 + (1 - core), pool), device_id_type=MESH,
        )
        c.start()
        pending.append(c)
    for t in turns:
        b = (b_own + t) % 4
        own = nn(feats_t[0, pl.ds(pl.multiple_of(b * 256, 256), 256), :], gp)
        pltpu.make_async_remote_copy(
            src_ref=core_send.at[b], dst_ref=core_recv.at[b],
            send_sem=c_ssem.at[b], recv_sem=c_rsem.at[b],
            device_id=(dp, pool), device_id_type=MESH,
        ).wait_recv()
        own = own + core_recv[b].astype(jnp.float32)
        for q in range(4):
            keep2[b, q] = own[q * 64:(q + 1) * 64]
            send2[b, q] = own[q * 64:(q + 1) * 64].astype(send2.dtype)
        for u in (2, 1, 3):
            a = (a_own + u) % 4
            ty = a * (1 - core) + y * core
            tx = x * (1 - core) + a * core
            c = pltpu.make_async_remote_copy(
                src_ref=send2.at[b, a], dst_ref=recv2.at[b, a_own],
                send_sem=s2_sem.at[b, a], recv_sem=r2_sem.at[b, a_own],
                device_id=(ty * 4 + zh * 2 + core, tx * 4 + z), device_id_type=MESH,
            )
            c.start()
            pending.append(c)
    for t in turns:
        b = (b_own + t) % 4
        part = keep2[b, a_own]
        for u in (1, 3, 2):
            a = (a_own + u) % 4
            pltpu.make_async_remote_copy(
                src_ref=send2.at[b, a], dst_ref=recv2.at[b, a],
                send_sem=s2_sem.at[b, a], recv_sem=r2_sem.at[b, a],
                device_id=(dp, pool), device_id_type=MESH,
            ).wait_recv()
            part = part + recv2[b, a].astype(jnp.float32)
        if t:
            send3[b] = part.astype(send3.dtype)
            ty = y * (1 - core) + b * core
            tx = b * (1 - core) + x * core
            c = pltpu.make_async_remote_copy(
                src_ref=send3.at[b], dst_ref=recv3.at[b_own],
                send_sem=s3_sem.at[b], recv_sem=r3_sem.at[b_own],
                device_id=(ty * 4 + zh * 2 + core, tx * 4 + z), device_id_type=MESH,
            )
            c.start()
            pending.append(c)
    for t in (1, 3, 2):
        b = (b_own + t) % 4
        pltpu.make_async_remote_copy(
            src_ref=send3.at[b], dst_ref=recv3.at[b],
            send_sem=s3_sem.at[b], recv_sem=r3_sem.at[b],
            device_id=(dp, pool), device_id_type=MESH,
        ).wait_recv()
        part = part + recv3[b].astype(jnp.float32)
    for q in range(8):
        send4[q] = part[q * 8:(q + 1) * 8]
    zz = zh * 4 + z
    for t in (4, 3, 5, 2, 6, 1, 7):
        q = (zz + t) % 8
        c = pltpu.make_async_remote_copy(
            src_ref=send4.at[q], dst_ref=recv4.at[zz],
            send_sem=s4_sem.at[q], recv_sem=r4_sem.at[zz],
            device_id=(y * 4 + (q // 4) * 2 + core, x * 4 + q % 4), device_id_type=MESH,
        )
        c.start()
        pending.append(c)
    result = send4[zz]
    for t in (1, 7, 2, 6, 3, 5, 4):
        q = (zz + t) % 8
        pltpu.make_async_remote_copy(
            src_ref=send4.at[q], dst_ref=recv4.at[q],
            send_sem=s4_sem.at[q], recv_sem=r4_sem.at[q],
            device_id=(dp, pool), device_id_type=MESH,
        ).wait_recv()
        result = result + recv4[q]
    out_ref[...] = result
    for c in inner:
        pl.when(middle)(c.wait_send)
    for c in pending:
        c.wait_send()


def per_device(feats, tower_w, partners, popularity_buckets, row_counts):
    f32, bf16, i32 = jnp.float32, jnp.bfloat16, jnp.int32
    vmem = pltpu.VMEM
    dma = pltpu.SemaphoreType.DMA
    return pl.pallas_call(
        kernel,
        out_shape=pltpu.VMEM((8, DE), f32),
        in_specs=[pl.BlockSpec(memory_space=pl.ANY)] * 5,
        out_specs=pl.BlockSpec(memory_space=pltpu.VMEM),
        scratch_shapes=[
            vmem((ROWS, DIN), bf16),
            vmem((DIN, DE), bf16),
            vmem((1, ROWS), i32),
            vmem((1, ROWS), i32),
            pltpu.SMEM((16, 16), i32),
            vmem((2, 1024, ROWS), bf16),
            vmem((16, ROWS, DE), bf16),
            vmem((16, ROWS, ROWS), f32),
            vmem((16, ROWS, ROWS), f32),
            vmem((16, 2, ROWS), f32),
            vmem((16, 1, ROWS), f32),
            vmem((ROWS, DE), f32),
            vmem((ROWS, 128), f32),
            vmem((ROWS, 128), f32),
            vmem((ROWS, 128), f32),
            vmem((ROWS, 128), f32),
            vmem((ROWS, 128), f32),
            vmem((ROWS, DE), f32),
            vmem((4, 256, DE), bf16),
            vmem((4, 256, DE), bf16),
            vmem((4, 4, 64, DE), f32),
            vmem((4, 4, 64, DE), bf16),
            vmem((4, 4, 64, DE), bf16),
            vmem((4, 64, DE), f32),
            vmem((4, 64, DE), f32),
            vmem((8, 8, DE), f32),
            vmem((8, 8, DE), f32),
            dma((KC, 2)),
            dma((3,)),
            dma((16,)),
            dma((16,)),
            dma((40,)),
            dma((16, 2)),
            dma((16,)),
            dma((16,)),
            dma((4,)),
            dma((4,)),
            dma((4, 4)),
            dma((4, 4)),
            dma((4,)),
            dma((4,)),
            dma((8,)),
            dma((8,)),
        ],
        compiler_params=pltpu.CompilerParams(collective_id=0, has_side_effects=True),
    )(feats, tower_w, partners.reshape(1, ROWS), popularity_buckets.reshape(1, ROWS), row_counts)


def solution(mesh):
    return jax.shard_map(
        per_device,
        mesh=mesh,
        in_specs=(P(("dp", "pool"), None), P(), P(("dp", "pool")), P(("dp", "pool")), P()),
        out_specs=P(("dp", "pool"), None),
        check_vma=False,
    )
```

```python
import functools

import jax
import jax.numpy as jnp
from jax import lax
from jax.experimental import pallas as pl
from jax.experimental.pallas import tpu as pltpu
from jax.sharding import PartitionSpec as P

MESH = pl.DeviceIdType.MESH
EPS = 1e-06
SCALE = 28.853900817779268
ROWS = 256
HALF = 128
DE = 256
DIN = 2048
KC = 4
KW = DIN // KC


def nt(left, right):
    return lax.dot_general(
        left, right, (((1,), (1,)), ((), ())), preferred_element_type=jnp.float32
    )


def nn(left, right):
    return jnp.dot(left, right, preferred_element_type=jnp.float32)


def kernel(
    feats_hbm, w_hbm, part_hbm, buck_hbm, counts_hbm, out_ref,
    feats_v, w_v, part_v, buck_v, counts_v, feats_t, e_all, a_all, b_all, meta, recips,
    normed_s, inv_s, own_w, own_part, own_valid, tot_s, g_s,
    core_send, core_recv, keep2, send2, recv2, send3, recv3, send4, recv4,
    in_sem, small_sem, meta_ssem, meta_rsem, e_ssem, e_rsem, r_ssem, r_rsem,
    c_ssem, c_rsem, s2_sem, r2_sem, s3_sem, r3_sem, s4_sem, r4_sem,
):
    dp = lax.axis_index("dp")
    pool = lax.axis_index("pool")
    y = dp // 4
    zh = (dp // 2) % 2
    core = dp % 2
    x = pool // 4
    z = pool % 4
    zs = [z, z + 1 - 2 * (z % 2), (z + 2) % 4, 3 - z]

    barrier = pltpu.get_barrier_semaphore()

    def greet(d, p):
        pl.semaphore_signal(barrier, inc=1, device_id=(d, p), device_id_type=MESH)

    for k in range(1, 16):
        greet(dp, (pool + k) % 16)
    greet(y * 4 + zh * 2 + (1 - core), pool)
    for k in range(1, 4):
        greet(((y + k) % 4) * 4 + zh * 2 + core, pool)
    for k in range(4):
        greet(y * 4 + (1 - zh) * 2 + core, x * 4 + k)

    loads = []
    for k in range(KC):
        cols = pl.ds(k * KW, KW)
        a = pltpu.make_async_copy(feats_hbm.at[:, cols], feats_v.at[:, cols], in_sem.at[k, 0])
        b = pltpu.make_async_copy(w_hbm.at[cols, :], w_v.at[cols, :], in_sem.at[k, 1])
        a.start()
        b.start()
        loads.append((a, b))
    small = [
        pltpu.make_async_copy(part_hbm, part_v, small_sem.at[0]),
        pltpu.make_async_copy(buck_hbm, buck_v, small_sem.at[1]),
        pltpu.make_async_copy(counts_hbm, counts_v, small_sem.at[2]),
    ]
    for c in small:
        c.start()

    projected = None
    for k in range(KC):
        loads[k][0].wait()
        loads[k][1].wait()
        cols = pl.ds(k * KW, KW)
        term = nn(feats_v[:, cols], w_v[cols, :])
        projected = term if projected is None else projected + term
    inv_norm = lax.rsqrt(jnp.sum(projected * projected, axis=1, keepdims=True) + EPS)
    normed = projected * inv_norm
    normed_s[...] = normed
    inv_s[...] = jnp.broadcast_to(inv_norm, (ROWS, 128))
    e_all[pool] = normed.astype(jnp.bfloat16)

    for c in small:
        c.wait()
    cnt = counts_v[dp, pool]
    lane = lax.broadcasted_iota(jnp.int32, (1, ROWS), 1)
    valid = lane < cnt
    part_l = jnp.where(valid, part_v[...], -1).astype(jnp.float32)
    w_l = jnp.where(valid, jnp.exp((buck_v[...].astype(jnp.float32) + 0.5) * 0.25), 0.0)
    meta[pool, 0:1, :] = part_l
    meta[pool, 1:2, :] = w_l

    pl.semaphore_wait(barrier, 23)

    pending = []

    def rows_of(h):
        return pl.ds(h * HALF, HALF)

    def send(slot, h, target, n):
        c = pltpu.make_async_remote_copy(
            src_ref=e_all.at[slot, rows_of(h)], dst_ref=e_all.at[slot, rows_of(h)],
            send_sem=e_ssem.at[n], recv_sem=e_rsem.at[slot, h],
            device_id=(dp, target), device_id_type=MESH,
        )
        c.start()
        pending.append(c)

    def arrive(slot, h):
        pltpu.make_async_remote_copy(
            src_ref=e_all.at[slot, rows_of(h)], dst_ref=e_all.at[slot, rows_of(h)],
            send_sem=e_ssem.at[0], recv_sem=e_rsem.at[slot, h],
            device_id=(dp, pool), device_id_type=MESH,
        ).wait_recv()

    def meta_arrive(slot):
        pltpu.make_async_remote_copy(
            src_ref=meta.at[slot], dst_ref=meta.at[slot],
            send_sem=meta_ssem.at[0], recv_sem=meta_rsem.at[slot],
            device_id=(dp, pool), device_id_type=MESH,
        ).wait_recv()

    right = (x + 1) % 4
    left = (x + 3) % 4
    far = (x + 2) % 4
    middle = z % 2 + z // 2 == 1
    count = iter(range(64))
    inner = []

    def copy_to_z(slot, h, c, n):
        return pltpu.make_async_remote_copy(
            src_ref=e_all.at[slot, rows_of(h)], dst_ref=e_all.at[slot, rows_of(h)],
            send_sem=e_ssem.at[n], recv_sem=e_rsem.at[slot, h],
            device_id=(dp, x * 4 + zs[c]), device_id_type=MESH,
        )

    def to_right(slot, h):
        send(slot, h, right * 4 + z, next(count))

    def to_left(slot, h):
        send(slot, h, left * 4 + z, next(count))

    def to_z(slot, h, c):
        send(slot, h, x * 4 + zs[c], next(count))

    for h in (0, 1):
        to_right(pool, h)
        to_left(pool, 1 - h)
        to_z(pool, h, 1)
    for h in (0, 1):
        to_z(pool, h, 2)
    for k in range(1, 16):
        c = pltpu.make_async_remote_copy(
            src_ref=meta.at[pool], dst_ref=meta.at[pool],
            send_sem=meta_ssem.at[k], recv_sem=meta_rsem.at[pool],
            device_id=(dp, (pool + k) % 16), device_id_type=MESH,
        )
        c.start()
        pending.append(c)

    own_part[...] = jnp.broadcast_to(part_l, (128, ROWS)).T
    own_w[...] = jnp.broadcast_to(w_l, (128, ROWS)).T
    own_valid[...] = jnp.broadcast_to(jnp.where(valid, 1.0, 0.0), (128, ROWS)).T

    def wide(v):
        return jnp.concatenate([v, v], axis=1)

    def scores(slot, first=False):
        s = nt(e_all[pool], e_all[slot])
        e = jnp.exp2(s * SCALE)
        if first:
            ri = lax.broadcasted_iota(jnp.int32, (ROWS, ROWS), 0)
            ci = lax.broadcasted_iota(jnp.int32, (ROWS, ROWS), 1)
            e = jnp.where(ri == ci, 0.0, e)
        b_all[slot] = e * wide(own_w[...])
        t = e * meta[slot, 1:2, :]
        a_all[slot] = t
        t = t[:, :128] + t[:, 128:]
        if first:
            tot_s[...] = t
        else:
            tot_s[...] += t

    scores(pool, True)

    def transposes(lo, hi):
        for m in range(lo, hi):
            my, mz, mc = m // 4, (m // 2) % 2, m % 2
            t = feats_v[:, m * 128:(m + 1) * 128].T
            which = (mc + core) % 2
            for mx in range(4):
                at = (my * (2 + 6 * mc) + mx * (8 - 6 * mc) + mz) * 32
                feats_t[which, at:at + 32, :] = t[mx * 32:(mx + 1) * 32]

    transposes(0, 8)

    def member(dx, c):
        return ((x + dx) % 4) * 4 + zs[c]

    def take(slot):
        meta_arrive(slot)
        scores(slot)

    def turn(c):
        arrive(member(3, c), 0)
        to_right(member(3, c), 0)
        arrive(member(1, c), 1)
        to_left(member(1, c), 1)

    def spread(c):
        for h in (0, 1):
            arrive(member(0, c), h)
            to_right(member(0, c), h)
            to_left(member(0, c), h)

    def rest(c):
        arrive(member(3, c), 1)
        take(member(3, c))
        arrive(member(1, c), 0)
        take(member(1, c))

    turn(0)
    spread(1)
    second, across = member(0, 2), member(2, 0)
    to_end = [copy_to_z(second, h, 1, 30 + h) for h in (0, 1)]
    to_other = [copy_to_z(pool, h, 3, 32 + h) for h in (0, 1)]
    inner += to_end + to_other
    second_x = []
    for h in (0, 1):
        for side in (right, left):
            second_x.append(pltpu.make_async_remote_copy(
                src_ref=e_all.at[second, rows_of(h)], dst_ref=e_all.at[second, rows_of(h)],
                send_sem=e_ssem.at[34 + len(second_x)], recv_sem=e_rsem.at[second, h],
                device_id=(dp, side * 4 + z), device_id_type=MESH,
            ))
    across_z = [copy_to_z(across, h, c, 38 + 2 * h + c // 2) for h in (0, 1) for c in (1, 3)]
    pending += second_x + across_z

    def send_second(h, relay):
        arrive(second, h)
        if relay:
            to_end[h].start()
        second_x[2 * h].start()
        second_x[2 * h + 1].start()

    def send_across(h):
        arrive(across, h)
        across_z[2 * h].start()
        across_z[2 * h + 1].start()

    @pl.when(middle)
    def _():
        for cp in to_other:
            cp.start()
        for h in (0, 1):
            send_second(h, True)
        for h in (0, 1):
            send_across(h)

    @pl.when(jnp.logical_not(middle))
    def _():
        for h in (0, 1):
            send_across(h)
        for h in (0, 1):
            send_second(h, False)

    transposes(8, 16)
    take(member(0, 1))
    rest(0)
    take(across)
    take(second)
    for h in (0, 1):
        arrive(member(3, 1), h)
        arrive(member(1, 1), h)
    take(member(3, 1))
    take(member(1, 1))
    turn(2)
    spread(3)
    take(member(0, 3))
    rest(2)
    arrive(member(2, 1), 0)
    arrive(member(2, 1), 1)
    take(member(2, 1))
    arrive(member(2, 2), 0)
    arrive(member(2, 2), 1)
    take(member(2, 2))
    arrive(member(2, 3), 0)
    arrive(member(2, 3), 1)
    take(member(2, 3))
    for h in (0, 1):
        arrive(member(3, 3), h)
        arrive(member(1, 3), h)
    take(member(3, 3))
    take(member(1, 3))

    order = [
        [(2, 3), (2, 2), (2, 1), (3, 3)],
        [(1, 3), (3, 2), (1, 2), (2, 0)],
        [(3, 1), (1, 1), (0, 3), (0, 2)],
        [(3, 0), (1, 0), (0, 1), (0, 0)],
    ]

    total = jnp.broadcast_to(jnp.sum(tot_s[...], axis=1, keepdims=True), (ROWS, 128))
    recip_own = own_valid[...] / total
    recips[pool] = recip_own.T[0:1, :]
    n = 0
    for group in order:
        for dx, c in group:
            if (dx, c) == (0, 0):
                continue
            cp = pltpu.make_async_remote_copy(
                src_ref=recips.at[pool], dst_ref=recips.at[pool],
                send_sem=r_ssem.at[n], recv_sem=r_rsem.at[pool],
                device_id=(dp, member(dx, c)), device_id_type=MESH,
            )
            cp.start()
            pending.append(cp)
            n += 1

    tot_s[...] = recip_own
    g_s[...] = jnp.zeros_like(g_s)
    lane_f = lax.broadcasted_iota(jnp.int32, (1, ROWS), 1).astype(jnp.float32)

    def row_term(i, carry):
        acc = None
        for j in range(4):
            s = i * 4 + j
            hit = wide(own_part[...]) == lane_f + (s * ROWS).astype(jnp.float32)
            coef = a_all[s] * wide(tot_s[...])
            coef = jnp.where(hit, coef - 1.0, coef).astype(jnp.bfloat16)
            term = nn(coef, e_all[s])
            acc = term if acc is None else acc + term
        g_s[...] += acc
        return carry

    lax.fori_loop(0, 4, row_term, 0)

    mine = lax.broadcasted_iota(jnp.int32, (ROWS, 128), 0).astype(jnp.float32) + (pool * ROWS).astype(jnp.float32)
    own_part[...] = mine
    for group in order[::-1]:
        slots = [member(dx, c) for dx, c in group[::-1]]
        for (dx, c), s in zip(group[::-1], slots):
            if (dx, c) == (0, 0):
                continue
            pltpu.make_async_remote_copy(
                src_ref=recips.at[s], dst_ref=recips.at[s],
                send_sem=r_ssem.at[0], recv_sem=r_rsem.at[s],
                device_id=(dp, pool), device_id_type=MESH,
            ).wait_recv()
        acc = None
        for s in slots:
            hit = wide(own_part[...]) == meta[s, 0:1, :]
            coef = b_all[s] * recips[s]
            coef = jnp.where(hit, coef - 1.0, coef).astype(jnp.bfloat16)
            term = nn(coef, e_all[s])
            acc = term if acc is None else acc + term
        g_s[...] += acc

    g = g_s[...]
    nrm = normed_s[...]
    g = (g - nrm * jnp.sum(nrm * g, axis=1, keepdims=True)) * wide(inv_s[...])
    gp = g.astype(jnp.bfloat16)

    a_own = y * (1 - core) + x * core
    b_own = x * (1 - core) + y * core
    turns = (2, 1, 3, 0)
    for t in turns:
        b = (a_own + t) % 4
        core_send[b] = nn(feats_t[1, pl.ds(pl.multiple_of(b * 256, 256), 256), :], gp).astype(core_send.dtype)
        c = pltpu.make_async_remote_copy(
            src_ref=core_send.at[b], dst_ref=core_recv.at[b],
            send_sem=c_ssem.at[b], recv_sem=c_rsem.at[b],
            device_id=(y * 4 + zh * 2 + (1 - core), pool), device_id_type=MESH,
        )
        c.start()
        pending.append(c)
    for t in turns:
        b = (b_own + t) % 4
        own = nn(feats_t[0, pl.ds(pl.multiple_of(b * 256, 256), 256), :], gp)
        pltpu.make_async_remote_copy(
            src_ref=core_send.at[b], dst_ref=core_recv.at[b],
            send_sem=c_ssem.at[b], recv_sem=c_rsem.at[b],
            device_id=(dp, pool), device_id_type=MESH,
        ).wait_recv()
        own = own + core_recv[b].astype(jnp.float32)
        for q in range(4):
            keep2[b, q] = own[q * 64:(q + 1) * 64]
            send2[b, q] = own[q * 64:(q + 1) * 64].astype(send2.dtype)
        for u in (2, 1, 3):
            a = (a_own + u) % 4
            ty = a * (1 - core) + y * core
            tx = x * (1 - core) + a * core
            c = pltpu.make_async_remote_copy(
                src_ref=send2.at[b, a], dst_ref=recv2.at[b, a_own],
                send_sem=s2_sem.at[b, a], recv_sem=r2_sem.at[b, a_own],
                device_id=(ty * 4 + zh * 2 + core, tx * 4 + z), device_id_type=MESH,
            )
            c.start()
            pending.append(c)
    for t in turns:
        b = (b_own + t) % 4
        part = keep2[b, a_own]
        for u in (1, 3, 2):
            a = (a_own + u) % 4
            pltpu.make_async_remote_copy(
                src_ref=send2.at[b, a], dst_ref=recv2.at[b, a],
                send_sem=s2_sem.at[b, a], recv_sem=r2_sem.at[b, a],
                device_id=(dp, pool), device_id_type=MESH,
            ).wait_recv()
            part = part + recv2[b, a].astype(jnp.float32)
        if t:
            send3[b] = part.astype(send3.dtype)
            ty = y * (1 - core) + b * core
            tx = b * (1 - core) + x * core
            c = pltpu.make_async_remote_copy(
                src_ref=send3.at[b], dst_ref=recv3.at[b_own],
                send_sem=s3_sem.at[b], recv_sem=r3_sem.at[b_own],
                device_id=(ty * 4 + zh * 2 + core, tx * 4 + z), device_id_type=MESH,
            )
            c.start()
            pending.append(c)
    for t in (1, 3, 2):
        b = (b_own + t) % 4
        pltpu.make_async_remote_copy(
            src_ref=send3.at[b], dst_ref=recv3.at[b],
            send_sem=s3_sem.at[b], recv_sem=r3_sem.at[b],
            device_id=(dp, pool), device_id_type=MESH,
        ).wait_recv()
        part = part + recv3[b].astype(jnp.float32)
    for q in range(8):
        send4[q] = part[q * 8:(q + 1) * 8]
    zz = zh * 4 + z
    for t in (4, 3, 5, 2, 6, 1, 7):
        q = (zz + t) % 8
        c = pltpu.make_async_remote_copy(
            src_ref=send4.at[q], dst_ref=recv4.at[zz],
            send_sem=s4_sem.at[q], recv_sem=r4_sem.at[zz],
            device_id=(y * 4 + (q // 4) * 2 + core, x * 4 + q % 4), device_id_type=MESH,
        )
        c.start()
        pending.append(c)
    result = send4[zz]
    for t in (1, 7, 2, 6, 3, 5, 4):
        q = (zz + t) % 8
        pltpu.make_async_remote_copy(
            src_ref=send4.at[q], dst_ref=recv4.at[q],
            send_sem=s4_sem.at[q], recv_sem=r4_sem.at[q],
            device_id=(dp, pool), device_id_type=MESH,
        ).wait_recv()
        result = result + recv4[q]
    out_ref[...] = result
    for c in inner:
        pl.when(middle)(c.wait_send)
    for c in pending:
        c.wait_send()


def per_device(feats, tower_w, partners, popularity_buckets, row_counts):
    f32, bf16, i32 = jnp.float32, jnp.bfloat16, jnp.int32
    vmem = pltpu.VMEM
    dma = pltpu.SemaphoreType.DMA
    return pl.pallas_call(
        kernel,
        out_shape=pltpu.VMEM((8, DE), f32),
        in_specs=[pl.BlockSpec(memory_space=pl.ANY)] * 5,
        out_specs=pl.BlockSpec(memory_space=pltpu.VMEM),
        scratch_shapes=[
            vmem((ROWS, DIN), bf16),
            vmem((DIN, DE), bf16),
            vmem((1, ROWS), i32),
            vmem((1, ROWS), i32),
            pltpu.SMEM((16, 16), i32),
            vmem((2, 1024, ROWS), bf16),
            vmem((16, ROWS, DE), bf16),
            vmem((16, ROWS, ROWS), f32),
            vmem((16, ROWS, ROWS), f32),
            vmem((16, 2, ROWS), f32),
            vmem((16, 1, ROWS), f32),
            vmem((ROWS, DE), f32),
            vmem((ROWS, 128), f32),
            vmem((ROWS, 128), f32),
            vmem((ROWS, 128), f32),
            vmem((ROWS, 128), f32),
            vmem((ROWS, 128), f32),
            vmem((ROWS, DE), f32),
            vmem((4, 256, DE), bf16),
            vmem((4, 256, DE), bf16),
            vmem((4, 4, 64, DE), f32),
            vmem((4, 4, 64, DE), bf16),
            vmem((4, 4, 64, DE), bf16),
            vmem((4, 64, DE), f32),
            vmem((4, 64, DE), f32),
            vmem((8, 8, DE), f32),
            vmem((8, 8, DE), f32),
            dma((KC, 2)),
            dma((3,)),
            dma((16,)),
            dma((16,)),
            dma((42,)),
            dma((16, 2)),
            dma((16,)),
            dma((16,)),
            dma((4,)),
            dma((4,)),
            dma((4, 4)),
            dma((4, 4)),
            dma((4,)),
            dma((4,)),
            dma((8,)),
            dma((8,)),
        ],
        compiler_params=pltpu.CompilerParams(collective_id=0, has_side_effects=True),
    )(feats, tower_w, partners.reshape(1, ROWS), popularity_buckets.reshape(1, ROWS), row_counts)


def solution(mesh):
    return jax.shard_map(
        per_device,
        mesh=mesh,
        in_specs=(P(("dp", "pool"), None), P(), P(("dp", "pool")), P(("dp", "pool")), P()),
        out_specs=P(("dp", "pool"), None),
        check_vma=False,
    )
```

```python
import functools

import jax
import jax.numpy as jnp
from jax import lax
from jax.experimental import pallas as pl
from jax.experimental.pallas import tpu as pltpu
from jax.sharding import PartitionSpec as P

MESH = pl.DeviceIdType.MESH
EPS = 1e-06
SCALE = 28.853900817779268
ROWS = 256
HALF = 128
DE = 256
DIN = 2048
KC = 4
KW = DIN // KC


def nt(left, right):
    return lax.dot_general(
        left, right, (((1,), (1,)), ((), ())), preferred_element_type=jnp.float32
    )


def nn(left, right):
    return jnp.dot(left, right, preferred_element_type=jnp.float32)


def kernel(
    feats_hbm, w_hbm, part_hbm, buck_hbm, counts_hbm, out_ref,
    feats_v, w_v, part_v, buck_v, counts_v, feats_t, e_all, a_all, b_all, meta, recips,
    normed_s, inv_s, own_w, own_part, own_valid, tot_s, g_s,
    core_send, core_recv, keep2, send2, recv2, send3, recv3, send4, recv4,
    in_sem, small_sem, out_sem, m_sem, e_sem, r_sem, c_sem, r2_sem, r3_sem, r4_sem,
):
    dp = lax.axis_index("dp")
    pool = lax.axis_index("pool")
    y = dp // 4
    zh = (dp // 2) % 2
    core = dp % 2
    x = pool // 4
    z = pool % 4
    zs = [z, z + 1 - 2 * (z % 2), (z + 2) % 4, 3 - z]
    middle = z % 2 + z // 2 == 1
    right = (x + 1) % 4
    left = (x + 3) % 4

    def member(dx, c):
        return ((x + dx) % 4) * 4 + zs[c]

    S_META, S_COL, S_E, S_MID, S_RECIP, S_CORE, S_TWO, S_THREE, S_FOUR = range(9)

    def remote(src, dst, kind, sem, d, p):
        return pltpu.make_async_remote_copy(
            src_ref=src, dst_ref=dst, send_sem=out_sem.at[kind], recv_sem=sem,
            device_id=(d, p), device_id_type=MESH,
        )

    def landed(ref, sem):
        remote(ref, ref, 0, sem, dp, pool).wait_recv()

    barrier = pltpu.get_barrier_semaphore()

    def greet(d, p):
        pl.semaphore_signal(barrier, inc=1, device_id=(d, p), device_id_type=MESH)

    for k in range(1, 16):
        greet(dp, (pool + k) % 16)
    greet(y * 4 + zh * 2 + (1 - core), pool)
    for k in range(1, 4):
        greet(((y + k) % 4) * 4 + zh * 2 + core, pool)
    for k in range(4):
        greet(y * 4 + (1 - zh) * 2 + core, x * 4 + k)

    for k in range(KC):
        cols = pl.ds(k * KW, KW)
        pltpu.make_async_copy(feats_hbm.at[:, cols], feats_v.at[:, cols], in_sem.at[k]).start()
        pltpu.make_async_copy(w_hbm.at[cols, :], w_v.at[cols, :], in_sem.at[k]).start()
    small = [
        pltpu.make_async_copy(part_hbm, part_v, small_sem.at[0]),
        pltpu.make_async_copy(buck_hbm, buck_v, small_sem.at[1]),
        pltpu.make_async_copy(counts_hbm, counts_v, small_sem.at[2]),
    ]
    for c in small:
        c.start()

    projected = None
    for k in range(KC):
        both = pl.ds(0, 2 * KW)
        pltpu.make_async_copy(w_hbm.at[both, :], w_v.at[both, :], in_sem.at[k]).wait()
        cols = pl.ds(k * KW, KW)
        term = nn(feats_v[:, cols], w_v[cols, :])
        projected = term if projected is None else projected + term
    inv_norm = lax.rsqrt(jnp.sum(projected * projected, axis=1, keepdims=True) + EPS)
    normed = projected * inv_norm
    normed_s[...] = normed
    inv_s[...] = jnp.broadcast_to(inv_norm, (ROWS, 128))
    e_all[pool] = normed.astype(jnp.bfloat16)

    for c in small:
        c.wait()
    cnt = counts_v[dp, pool]
    lane = lax.broadcasted_iota(jnp.int32, (1, ROWS), 1)
    valid = lane < cnt
    part_l = jnp.where(valid, part_v[...], -1).astype(jnp.float32)
    w_l = jnp.where(valid, jnp.exp((buck_v[...].astype(jnp.float32) + 0.5) * 0.25), 0.0)
    meta[pool, 0:1, :] = part_l
    meta[pool, 1:2, :] = w_l

    pl.semaphore_wait(barrier, 23)

    for c in (1, 2, 3):
        remote(meta.at[pool], meta.at[pool], S_META, m_sem.at[0], dp, member(0, c)).start()

    def rows_of(h):
        return pl.ds(h * HALF, HALF)

    def sem_of(dx, c, h):
        if dx == 0:
            return e_sem.at[2 * (c - 1) + h]
        if dx == 2:
            return e_sem.at[6 + h] if c == 0 else e_sem.at[15 + c]
        if c % 2:
            return e_sem.at[14 + c // 2]
        onward = h == (0 if dx == 3 else 1)
        return e_sem.at[(8 if c == 0 else 11) + (1 if not onward else 0 if dx == 3 else 2)]

    def copy(dx, c, h, side, kind=S_E):
        slot = member(dx, c)
        half = e_all.at[slot, rows_of(h)]
        if side == "right":
            return remote(half, half, kind, sem_of((dx + 3) % 4, c, h), dp, right * 4 + z)
        if side == "left":
            return remote(half, half, kind, sem_of((dx + 1) % 4, c, h), dp, left * 4 + z)
        return remote(half, half, kind, sem_of(dx, c ^ side, h), dp, x * 4 + zs[side])

    def arrive(dx, c, h):
        landed(e_all.at[member(dx, c), rows_of(h)], sem_of(dx, c, h))

    for h in (0, 1):
        copy(0, 0, h, "right").start()
        copy(0, 0, 1 - h, "left").start()
        copy(0, 0, h, 1).start()

    @pl.when(jnp.logical_not(middle))
    def _():
        for h in (0, 1):
            copy(0, 0, h, 2).start()

    own_part[...] = jnp.broadcast_to(part_l, (128, ROWS)).T
    own_w[...] = jnp.broadcast_to(w_l, (128, ROWS)).T
    own_valid[...] = jnp.broadcast_to(jnp.where(valid, 1.0, 0.0), (128, ROWS)).T

    def wide(v):
        return jnp.concatenate([v, v], axis=1)

    def scores(dx, c):
        slot = member(dx, c)
        s = nt(e_all[pool], e_all[slot])
        e = jnp.exp2(s * SCALE)
        if (dx, c) == (0, 0):
            ri = lax.broadcasted_iota(jnp.int32, (ROWS, ROWS), 0)
            ci = lax.broadcasted_iota(jnp.int32, (ROWS, ROWS), 1)
            e = jnp.where(ri == ci, 0.0, e)
        b_all[slot] = e * wide(own_w[...])
        t = e * meta[slot, 1:2, :]
        a_all[slot] = t
        t = t[:, :128] + t[:, 128:]
        if (dx, c) == (0, 0):
            tot_s[...] = t
        else:
            tot_s[...] += t

    scores(0, 0)

    def transposes(lo, hi):
        for m in range(lo, hi):
            my, mz, mc = m // 4, (m // 2) % 2, m % 2
            t = feats_v[:, m * 128:(m + 1) * 128].T
            which = (mc + core) % 2
            for mx in range(4):
                at = (my * (2 + 6 * mc) + mx * (8 - 6 * mc) + mz) * 32
                feats_t[which, at:at + 32, :] = t[mx * 32:(mx + 1) * 32]

    transposes(0, 16)

    @pl.when(middle)
    def _():
        for h in (0, 1):
            copy(0, 0, h, 2).start()

    def spread(c):
        for h in (0, 1):
            arrive(0, c, h)
            copy(0, c, h, "right").start()
            copy(0, c, h, "left").start()

    def rest(c):
        landed(e_all.at[member(3, c)], sem_of(3, c, 1))
        scores(3, c)
        scores(1, c)

    arrive(3, 0, 0)
    copy(3, 0, 0, "right").start()

    arrive(1, 0, 1)
    copy(1, 0, 1, "left").start()
    column = meta.at[pl.ds(x * 4, 4)]
    landed(meta.at[0:3], m_sem.at[0])
    for dx in (1, 3, 2):
        remote(column, column, S_COL, m_sem.at[1], dp, member(dx, 0)).start()
    spread(1)

    def send_second(relay):
        for h in (0, 1):
            arrive(0, 2, h)
            if relay:
                copy(0, 2, h, 1, S_MID).start()
            copy(0, 2, h, "right").start()
            copy(0, 2, h, "left").start()

    def send_across():
        for h in (0, 1):
            arrive(2, 0, h)
            copy(2, 0, h, 1).start()
            copy(2, 0, h, 3).start()

    @pl.when(middle)
    def _():
        for h in (0, 1):
            copy(0, 0, h, 3, S_MID).start()
        send_second(True)
        send_across()

    @pl.when(jnp.logical_not(middle))
    def _():
        send_across()
        send_second(False)

    scores(0, 1)
    landed(meta.at[0:12], m_sem.at[1])
    rest(0)
    scores(2, 0)
    scores(0, 2)
    landed(e_all.at[0:2], sem_of(3, 1, 0))
    scores(3, 1)
    scores(1, 1)
    arrive(3, 2, 0)
    copy(3, 2, 0, "right").start()
    arrive(1, 2, 1)
    copy(1, 2, 1, "left").start()
    spread(3)
    scores(0, 3)
    rest(2)
    for c in (1, 2, 3):
        landed(e_all.at[member(2, c)], sem_of(2, c, 0))
        scores(2, c)
    landed(e_all.at[0:2], sem_of(3, 3, 0))
    scores(3, 3)
    scores(1, 3)

    near = [
        [(0, 0), (0, 1), (1, 0), (3, 0)],
        [(0, 2), (0, 3), (1, 1), (3, 1)],
        [(2, 0), (1, 2), (3, 2), (1, 3), (3, 3)],
        [(2, 1), (2, 2), (2, 3)],
    ]
    total = jnp.broadcast_to(jnp.sum(tot_s[...], axis=1, keepdims=True), (ROWS, 128))
    recip_own = own_valid[...] / total
    recips[pool] = recip_own.T[0:1, :]
    for n, group in reversed(list(enumerate(near))):
        for dx, c in reversed(group):
            if (dx, c) != (0, 0):
                remote(recips.at[pool], recips.at[pool], S_RECIP, r_sem.at[n], dp, member(dx, c)).start()

    tot_s[...] = recip_own
    g_s[...] = jnp.zeros_like(g_s)
    lane_f = lax.broadcasted_iota(jnp.int32, (1, ROWS), 1).astype(jnp.float32)

    def row_term(i, carry):
        acc = None
        for j in range(4):
            s = i * 4 + j
            hit = wide(own_part[...]) == lane_f + (s * ROWS).astype(jnp.float32)
            coef = a_all[s] * wide(tot_s[...])
            coef = jnp.where(hit, coef - 1.0, coef).astype(jnp.bfloat16)
            term = nn(coef, e_all[s])
            acc = term if acc is None else acc + term
        g_s[...] += acc
        return carry

    lax.fori_loop(0, 4, row_term, 0)

    mine = lax.broadcasted_iota(jnp.int32, (ROWS, 128), 0).astype(jnp.float32) + (pool * ROWS).astype(jnp.float32)
    own_part[...] = mine
    for n, group in enumerate(near):
        landed(recips.at[0:len(group) - (n == 0)], r_sem.at[n])
        acc = None
        for dx, c in group:
            s = member(dx, c)
            hit = wide(own_part[...]) == meta[s, 0:1, :]
            coef = b_all[s] * recips[s]
            coef = jnp.where(hit, coef - 1.0, coef).astype(jnp.bfloat16)
            term = nn(coef, e_all[s])
            acc = term if acc is None else acc + term
        g_s[...] += acc

    g = g_s[...]
    nrm = normed_s[...]
    g = (g - nrm * jnp.sum(nrm * g, axis=1, keepdims=True)) * wide(inv_s[...])
    gp = g.astype(jnp.bfloat16)

    a_own = y * (1 - core) + x * core
    b_own = x * (1 - core) + y * core
    turns = (2, 1, 3, 0)
    for t in turns:
        b = (a_own + t) % 4
        core_send[b] = nn(feats_t[1, pl.ds(pl.multiple_of(b * 256, 256), 256), :], gp).astype(core_send.dtype)
        remote(
            core_send.at[b], core_recv.at[b], S_CORE, c_sem.at[b], y * 4 + zh * 2 + (1 - core), pool
        ).start()
    for t in turns:
        b = (b_own + t) % 4
        own = nn(feats_t[0, pl.ds(pl.multiple_of(b * 256, 256), 256), :], gp)
        landed(core_recv.at[b], c_sem.at[b])
        own = own + core_recv[b].astype(jnp.float32)
        for q in range(4):
            keep2[b, q] = own[q * 64:(q + 1) * 64]
            send2[b, q] = own[q * 64:(q + 1) * 64].astype(send2.dtype)
        for u in (2, 1, 3):
            a = (a_own + u) % 4
            ty = a * (1 - core) + y * core
            tx = x * (1 - core) + a * core
            remote(
                send2.at[b, a], recv2.at[b, a_own], S_TWO, r2_sem.at[b], ty * 4 + zh * 2 + core, tx * 4 + z
            ).start()
    for t in turns:
        b = (b_own + t) % 4
        part = keep2[b, a_own]
        landed(recv2.at[b, 0:3], r2_sem.at[b])
        for u in (1, 3, 2):
            part = part + recv2[b, (a_own + u) % 4].astype(jnp.float32)
        if t:
            send3[b] = part.astype(send3.dtype)
            ty = y * (1 - core) + b * core
            tx = b * (1 - core) + x * core
            remote(
                send3.at[b], recv3.at[b_own], S_THREE, r3_sem.at[0], ty * 4 + zh * 2 + core, tx * 4 + z
            ).start()
    landed(recv3.at[0:3], r3_sem.at[0])
    for t in (1, 3, 2):
        part = part + recv3[(b_own + t) % 4].astype(jnp.float32)
    for q in range(8):
        send4[q] = part[q * 8:(q + 1) * 8]
    zz = zh * 4 + z
    for t in (4, 3, 5, 2, 6, 1, 7):
        q = (zz + t) % 8
        remote(
            send4.at[q], recv4.at[zz], S_FOUR, r4_sem.at[0], y * 4 + (q // 4) * 2 + core, x * 4 + q % 4
        ).start()
    result = send4[zz]
    landed(recv4.at[0:7], r4_sem.at[0])
    for t in (1, 7, 2, 6, 3, 5, 4):
        result = result + recv4[(zz + t) % 8]
    out_ref[...] = result

    def sent(ref, kind):
        remote(ref, ref, kind, r4_sem.at[0], dp, pool).wait_send()

    sent(meta.at[0:3], S_META)
    sent(meta.at[0:12], S_COL)
    sent(e_all.at[0:14], S_E)
    pl.when(middle)(lambda: sent(e_all.at[0:2], S_MID))
    sent(recips.at[0:15], S_RECIP)
    sent(core_send, S_CORE)
    sent(send2.at[0:3], S_TWO)
    sent(send3.at[0:3], S_THREE)
    sent(send4.at[0:7], S_FOUR)


def per_device(feats, tower_w, partners, popularity_buckets, row_counts):
    f32, bf16, i32 = jnp.float32, jnp.bfloat16, jnp.int32
    vmem = pltpu.VMEM
    dma = pltpu.SemaphoreType.DMA
    return pl.pallas_call(
        kernel,
        out_shape=pltpu.VMEM((8, DE), f32),
        in_specs=[pl.BlockSpec(memory_space=pl.ANY)] * 5,
        out_specs=pl.BlockSpec(memory_space=pltpu.VMEM),
        scratch_shapes=[
            vmem((ROWS, DIN), bf16),
            vmem((DIN, DE), bf16),
            vmem((1, ROWS), i32),
            vmem((1, ROWS), i32),
            pltpu.SMEM((16, 16), i32),
            vmem((2, 1024, ROWS), bf16),
            vmem((16, ROWS, DE), bf16),
            vmem((16, ROWS, ROWS), f32),
            vmem((16, ROWS, ROWS), f32),
            vmem((16, 2, ROWS), f32),
            vmem((16, 1, ROWS), f32),
            vmem((ROWS, DE), f32),
            vmem((ROWS, 128), f32),
            vmem((ROWS, 128), f32),
            vmem((ROWS, 128), f32),
            vmem((ROWS, 128), f32),
            vmem((ROWS, 128), f32),
            vmem((ROWS, DE), f32),
            vmem((4, 256, DE), bf16),
            vmem((4, 256, DE), bf16),
            vmem((4, 4, 64, DE), f32),
            vmem((4, 4, 64, DE), bf16),
            vmem((4, 4, 64, DE), bf16),
            vmem((4, 64, DE), f32),
            vmem((4, 64, DE), f32),
            vmem((8, 8, DE), f32),
            vmem((8, 8, DE), f32),
            dma((KC,)),
            dma((3,)),
            dma((9,)),
            dma((2,)),
            dma((19,)),
            dma((4,)),
            dma((4,)),
            dma((4,)),
            dma((1,)),
            dma((1,)),
        ],
        compiler_params=pltpu.CompilerParams(collective_id=0, has_side_effects=True),
    )(feats, tower_w, partners.reshape(1, ROWS), popularity_buckets.reshape(1, ROWS), row_counts)


def solution(mesh):
    return jax.shard_map(
        per_device,
        mesh=mesh,
        in_specs=(P(("dp", "pool"), None), P(), P(("dp", "pool")), P(("dp", "pool")), P()),
        out_specs=P(("dp", "pool"), None),
        check_vma=False,
    )
```

```python
import functools

import jax
import jax.numpy as jnp
from jax import lax
from jax.experimental import pallas as pl
from jax.experimental.pallas import tpu as pltpu
from jax.sharding import PartitionSpec as P

MESH = pl.DeviceIdType.MESH
EPS = 1e-06
SCALE = 28.853900817779268
ROWS = 256
HALF = 128
DE = 256
DIN = 2048
KC = 4
KW = DIN // KC


def nt(left, right):
    return lax.dot_general(
        left, right, (((1,), (1,)), ((), ())), preferred_element_type=jnp.float32
    )


def nn(left, right):
    return jnp.dot(left, right, preferred_element_type=jnp.float32)


def kernel(
    feats_hbm, w_hbm, part_hbm, buck_hbm, counts_hbm, out_ref,
    feats_v, w_v, part_v, buck_v, counts_v, feats_t, e_all, a_all, b_all, meta, recips,
    normed_s, inv_s, own_w, own_part, own_valid, tot_s, g_s, size,
    core_send, core_recv, keep2, send2, recv2, send3, recv3, send4, recv4,
    in_sem, small_sem, out_sem, e_sem, r_sem, c_sem, r2_sem, r3_sem, r4_sem,
):
    dp = lax.axis_index("dp")
    pool = lax.axis_index("pool")
    y = dp // 4
    zh = (dp // 2) % 2
    core = dp % 2
    x = pool // 4
    z = pool % 4
    zs = [z, z + 1 - 2 * (z % 2), (z + 2) % 4, 3 - z]
    middle = z % 2 + z // 2 == 1
    right = (x + 1) % 4
    left = (x + 3) % 4

    def member(dx, c):
        return ((x + dx) % 4) * 4 + zs[c]

    S_META, S_MIDMETA, S_E, S_MID, S_RECIP, S_CORE, S_TWO, S_THREE, S_FOUR = range(9)

    def remote(src, dst, kind, sem, d, p):
        return pltpu.make_async_remote_copy(
            src_ref=src, dst_ref=dst, send_sem=out_sem.at[kind], recv_sem=sem,
            device_id=(d, p), device_id_type=MESH,
        )

    def landed(ref, sem):
        remote(ref, ref, 0, sem, dp, pool).wait_recv()

    barrier = pltpu.get_barrier_semaphore()

    def greet(d, p):
        pl.semaphore_signal(barrier, inc=1, device_id=(d, p), device_id_type=MESH)

    zz = zh * 4 + z
    for k in (2, 6, 1, 7):
        q = (zz + k) % 8
        greet(y * 4 + (q // 4) * 2 + core, x * 4 + q % 4)
    for k in (2, 1, 3):
        greet(dp, ((x + k) % 4) * 4 + z)
        greet(((y + k) % 4) * 4 + zh * 2 + core, pool)
    greet(y * 4 + zh * 2 + (1 - core), pool)

    for k in range(KC):
        cols = pl.ds(k * KW, KW)
        pltpu.make_async_copy(feats_hbm.at[:, cols], feats_v.at[:, cols], in_sem.at[k]).start()
        pltpu.make_async_copy(w_hbm.at[cols, :], w_v.at[cols, :], in_sem.at[k]).start()
    small = [
        pltpu.make_async_copy(part_hbm, part_v, small_sem.at[0]),
        pltpu.make_async_copy(buck_hbm, buck_v, small_sem.at[1]),
        pltpu.make_async_copy(counts_hbm, counts_v, small_sem.at[2]),
    ]
    for c in small:
        c.start()

    projected = None
    for k in range(KC):
        both = pl.ds(0, 2 * KW)
        pltpu.make_async_copy(w_hbm.at[both, :], w_v.at[both, :], in_sem.at[k]).wait()
        cols = pl.ds(k * KW, KW)
        term = nn(feats_v[:, cols], w_v[cols, :])
        projected = term if projected is None else projected + term
    inv_norm = lax.rsqrt(jnp.sum(projected * projected, axis=1, keepdims=True) + EPS)
    normed = projected * inv_norm
    normed_s[...] = normed
    inv_s[...] = jnp.broadcast_to(inv_norm, (ROWS, 128))
    e_all[pool] = normed.astype(jnp.bfloat16)

    for c in small:
        c.wait()
    cnt = counts_v[dp, pool]
    lane = lax.broadcasted_iota(jnp.int32, (1, ROWS), 1)
    valid = lane < cnt
    part_l = jnp.where(valid, part_v[...], -1).astype(jnp.float32)
    w_l = jnp.where(valid, jnp.exp((buck_v[...].astype(jnp.float32) + 0.5) * 0.25), 0.0)
    meta[pool, 0:1, :] = part_l
    meta[pool, 1:2, :] = w_l

    pl.semaphore_wait(barrier, 11)

    def rows_of(h):
        return pl.ds(h * HALF, HALF)

    def sem_of(dx, c, h):
        if dx == 0:
            return e_sem.at[2 * (c - 1) + h]
        if dx == 2:
            return e_sem.at[6 + h] if c == 0 else e_sem.at[15 + c]
        if c % 2:
            return e_sem.at[14 + c // 2]
        onward = h == (0 if dx == 3 else 1)
        return e_sem.at[(8 if c == 0 else 11) + (1 if not onward else 0 if dx == 3 else 2)]

    def go(dx, c, h, side, middle_only=False):
        slot = member(dx, c)
        if side == "right":
            sem, target = sem_of((dx + 3) % 4, c, h), right * 4 + z
        elif side == "left":
            sem, target = sem_of((dx + 1) % 4, c, h), left * 4 + z
        else:
            sem, target = sem_of(dx, c ^ side, h), x * 4 + zs[side]
        half = e_all.at[slot, rows_of(h)]
        remote(half, half, S_MID if middle_only else S_E, sem, dp, target).start()
        if h:
            remote(
                meta.at[slot], meta.at[slot], S_MIDMETA if middle_only else S_META, sem, dp, target
            ).start()

    def arrive(dx, c, h):
        landed(size.at[0:32 + h], sem_of(dx, c, h))

    for h in (0, 1):
        go(0, 0, h, "right")
        go(0, 0, 1 - h, "left")
        go(0, 0, h, 1)

    @pl.when(jnp.logical_not(middle))
    def _():
        for h in (0, 1):
            go(0, 0, h, 2)

    own_part[...] = jnp.broadcast_to(part_l, (128, ROWS)).T
    own_w[...] = jnp.broadcast_to(w_l, (128, ROWS)).T
    own_valid[...] = jnp.broadcast_to(jnp.where(valid, 1.0, 0.0), (128, ROWS)).T

    def wide(v):
        return jnp.concatenate([v, v], axis=1)

    def scores(dx, c):
        slot = member(dx, c)
        s = nt(e_all[pool], e_all[slot])
        e = jnp.exp2(s * SCALE)
        if (dx, c) == (0, 0):
            ri = lax.broadcasted_iota(jnp.int32, (ROWS, ROWS), 0)
            ci = lax.broadcasted_iota(jnp.int32, (ROWS, ROWS), 1)
            e = jnp.where(ri == ci, 0.0, e)
        b_all[slot] = e * wide(own_w[...])
        t = e * meta[slot, 1:2, :]
        a_all[slot] = t
        t = t[:, :128] + t[:, 128:]
        if (dx, c) == (0, 0):
            tot_s[...] = t
        else:
            tot_s[...] += t

    scores(0, 0)

    def transposes(lo, hi):
        for m in range(lo, hi):
            my, mz, mc = m // 4, (m // 2) % 2, m % 2
            t = feats_v[:, m * 128:(m + 1) * 128].T
            which = (mc + core) % 2
            for mx in range(4):
                at = (my * (2 + 6 * mc) + mx * (8 - 6 * mc) + mz) * 32
                feats_t[which, at:at + 32, :] = t[mx * 32:(mx + 1) * 32]

    transposes(0, 16)

    @pl.when(middle)
    def _():
        for h in (0, 1):
            go(0, 0, h, 2)

    def spread(c):
        for h in (0, 1):
            arrive(0, c, h)
            go(0, c, h, "right")
            go(0, c, h, "left")

    def rest(c):
        landed(size.at[0:65], sem_of(3, c, 1))
        scores(3, c)
        scores(1, c)

    arrive(3, 0, 0)
    go(3, 0, 0, "right")

    arrive(1, 0, 1)
    go(1, 0, 1, "left")
    spread(1)

    def send_second(relay):
        for h in (0, 1):
            arrive(0, 2, h)
            if relay:
                go(0, 2, h, 1, True)
            go(0, 2, h, "right")
            go(0, 2, h, "left")

    def send_across():
        for h in (0, 1):
            arrive(2, 0, h)
            go(2, 0, h, 1)
            go(2, 0, h, 3)

    @pl.when(middle)
    def _():
        for h in (0, 1):
            go(0, 0, h, 3, True)
        send_second(True)
        send_across()

    @pl.when(jnp.logical_not(middle))
    def _():
        send_across()
        send_second(False)

    scores(0, 1)
    rest(0)
    scores(2, 0)
    scores(0, 2)
    landed(size.at[0:130], sem_of(3, 1, 0))
    scores(3, 1)
    scores(1, 1)
    arrive(3, 2, 0)
    go(3, 2, 0, "right")
    arrive(1, 2, 1)
    go(1, 2, 1, "left")
    spread(3)
    scores(0, 3)
    rest(2)
    for c in (1, 2, 3):
        landed(size.at[0:65], sem_of(2, c, 0))
        scores(2, c)
    landed(size.at[0:130], sem_of(3, 3, 0))
    scores(3, 3)
    scores(1, 3)

    near = [
        [(0, 0), (0, 1), (1, 0), (3, 0)],
        [(0, 2), (0, 3), (1, 1), (3, 1)],
        [(2, 0), (1, 2), (3, 2), (1, 3), (3, 3), (2, 1)],
        [(2, 2), (2, 3)],
    ]
    total = jnp.broadcast_to(jnp.sum(tot_s[...], axis=1, keepdims=True), (ROWS, 128))
    recip_own = own_valid[...] / total
    recips[pool] = recip_own.T[0:1, :]
    for n, group in reversed(list(enumerate(near))):
        for dx, c in reversed(group):
            if (dx, c) != (0, 0):
                remote(recips.at[pool], recips.at[pool], S_RECIP, r_sem.at[n], dp, member(dx, c)).start()

    tot_s[...] = recip_own
    g_s[...] = jnp.zeros_like(g_s)
    lane_f = lax.broadcasted_iota(jnp.int32, (1, ROWS), 1).astype(jnp.float32)

    def row_term(i, carry):
        acc = None
        for j in range(4):
            s = i * 4 + j
            hit = wide(own_part[...]) == lane_f + (s * ROWS).astype(jnp.float32)
            coef = a_all[s] * wide(tot_s[...])
            coef = jnp.where(hit, coef - 1.0, coef).astype(jnp.bfloat16)
            term = nn(coef, e_all[s])
            acc = term if acc is None else acc + term
        g_s[...] += acc
        return carry

    lax.fori_loop(0, 4, row_term, 0)

    mine = lax.broadcasted_iota(jnp.int32, (ROWS, 128), 0).astype(jnp.float32) + (pool * ROWS).astype(jnp.float32)
    own_part[...] = mine
    for n, group in enumerate(near):
        landed(recips.at[0:len(group) - (n == 0)], r_sem.at[n])
        acc = None
        for dx, c in group:
            s = member(dx, c)
            hit = wide(own_part[...]) == meta[s, 0:1, :]
            coef = b_all[s] * recips[s]
            coef = jnp.where(hit, coef - 1.0, coef).astype(jnp.bfloat16)
            term = nn(coef, e_all[s])
            acc = term if acc is None else acc + term
        g_s[...] += acc

    g = g_s[...]
    nrm = normed_s[...]
    g = (g - nrm * jnp.sum(nrm * g, axis=1, keepdims=True)) * wide(inv_s[...])
    gp = g.astype(jnp.bfloat16)

    a_own = y * (1 - core) + x * core
    b_own = x * (1 - core) + y * core
    turns = (2, 1, 3, 0)
    for t in turns:
        b = (a_own + t) % 4
        core_send[b] = nn(feats_t[1, pl.ds(pl.multiple_of(b * 256, 256), 256), :], gp).astype(core_send.dtype)
        remote(
            core_send.at[b], core_recv.at[b], S_CORE, c_sem.at[b], y * 4 + zh * 2 + (1 - core), pool
        ).start()
    for t in turns:
        b = (b_own + t) % 4
        own = nn(feats_t[0, pl.ds(pl.multiple_of(b * 256, 256), 256), :], gp)
        landed(core_recv.at[b], c_sem.at[b])
        own = own + core_recv[b].astype(jnp.float32)
        for q in range(4):
            keep2[b, q] = own[q * 64:(q + 1) * 64]
            send2[b, q] = own[q * 64:(q + 1) * 64].astype(send2.dtype)
        for u in (2, 1, 3):
            a = (a_own + u) % 4
            ty = a * (1 - core) + y * core
            tx = x * (1 - core) + a * core
            remote(
                send2.at[b, a], recv2.at[b, a_own], S_TWO, r2_sem.at[b], ty * 4 + zh * 2 + core, tx * 4 + z
            ).start()
    for t in turns:
        b = (b_own + t) % 4
        part = keep2[b, a_own]
        landed(recv2.at[b, 0:3], r2_sem.at[b])
        for u in (1, 3, 2):
            part = part + recv2[b, (a_own + u) % 4].astype(jnp.float32)
        if t:
            send3[b] = part.astype(send3.dtype)
            ty = y * (1 - core) + b * core
            tx = b * (1 - core) + x * core
            remote(
                send3.at[b], recv3.at[b_own], S_THREE, r3_sem.at[0], ty * 4 + zh * 2 + core, tx * 4 + z
            ).start()
    landed(recv3.at[0:3], r3_sem.at[0])
    for t in (1, 3, 2):
        part = part + recv3[(b_own + t) % 4].astype(jnp.float32)
    for q in range(8):
        send4[q] = part[q * 8:(q + 1) * 8]
    for t in (4, 3, 5, 2, 6, 1, 7):
        q = (zz + t) % 8
        remote(
            send4.at[q], recv4.at[zz], S_FOUR, r4_sem.at[0], y * 4 + (q // 4) * 2 + core, x * 4 + q % 4
        ).start()
    result = send4[zz]
    landed(recv4.at[0:7], r4_sem.at[0])
    for t in (1, 7, 2, 6, 3, 5, 4):
        result = result + recv4[(zz + t) % 8]
    out_ref[...] = result

    def sent(ref, kind):
        remote(ref, ref, kind, r4_sem.at[0], dp, pool).wait_send()

    sent(meta.at[0:14], S_META)
    pl.when(middle)(lambda: sent(meta.at[0:2], S_MIDMETA))
    sent(e_all.at[0:14], S_E)
    pl.when(middle)(lambda: sent(e_all.at[0:2], S_MID))
    sent(recips.at[0:15], S_RECIP)
    sent(core_send, S_CORE)
    sent(send2.at[0:3], S_TWO)
    sent(send3.at[0:3], S_THREE)
    sent(send4.at[0:7], S_FOUR)


def per_device(feats, tower_w, partners, popularity_buckets, row_counts):
    f32, bf16, i32 = jnp.float32, jnp.bfloat16, jnp.int32
    vmem = pltpu.VMEM
    dma = pltpu.SemaphoreType.DMA
    return pl.pallas_call(
        kernel,
        out_shape=pltpu.VMEM((8, DE), f32),
        in_specs=[pl.BlockSpec(memory_space=pl.ANY)] * 5,
        out_specs=pl.BlockSpec(memory_space=pltpu.VMEM),
        scratch_shapes=[
            vmem((ROWS, DIN), bf16),
            vmem((DIN, DE), bf16),
            vmem((1, ROWS), i32),
            vmem((1, ROWS), i32),
            pltpu.SMEM((16, 16), i32),
            vmem((2, 1024, ROWS), bf16),
            vmem((16, ROWS, DE), bf16),
            vmem((16, ROWS, ROWS), f32),
            vmem((16, ROWS, ROWS), f32),
            vmem((16, 2, ROWS), f32),
            vmem((16, 1, ROWS), f32),
            vmem((ROWS, DE), f32),
            vmem((ROWS, 128), f32),
            vmem((ROWS, 128), f32),
            vmem((ROWS, 128), f32),
            vmem((ROWS, 128), f32),
            vmem((ROWS, 128), f32),
            vmem((ROWS, DE), f32),
            vmem((130, 2, ROWS), f32),
            vmem((4, 256, DE), bf16),
            vmem((4, 256, DE), bf16),
            vmem((4, 4, 64, DE), f32),
            vmem((4, 4, 64, DE), bf16),
            vmem((4, 4, 64, DE), bf16),
            vmem((4, 64, DE), bf16),
            vmem((4, 64, DE), bf16),
            vmem((8, 8, DE), f32),
            vmem((8, 8, DE), f32),
            dma((KC,)),
            dma((3,)),
            dma((9,)),
            dma((19,)),
            dma((4,)),
            dma((4,)),
            dma((4,)),
            dma((1,)),
            dma((1,)),
        ],
        compiler_params=pltpu.CompilerParams(collective_id=0, has_side_effects=True),
    )(feats, tower_w, partners.reshape(1, ROWS), popularity_buckets.reshape(1, ROWS), row_counts)


def solution(mesh):
    return jax.shard_map(
        per_device,
        mesh=mesh,
        in_specs=(P(("dp", "pool"), None), P(), P(("dp", "pool")), P(("dp", "pool")), P()),
        out_specs=P(("dp", "pool"), None),
        check_vma=False,
    )
```

```python
import functools

import jax
import jax.numpy as jnp
from jax import lax
from jax.experimental import pallas as pl
from jax.experimental.pallas import tpu as pltpu
from jax.sharding import PartitionSpec as P

MESH = pl.DeviceIdType.MESH
EPS = 1e-06
SCALE = 28.853900817779268
ROWS = 256
HALF = 128
DE = 256
DIN = 2048
KC = 4
KW = DIN // KC


def nt(left, right):
    return lax.dot_general(
        left, right, (((1,), (1,)), ((), ())), preferred_element_type=jnp.float32
    )


def nn(left, right):
    return jnp.dot(left, right, preferred_element_type=jnp.float32)


def kernel(
    feats_hbm, w_hbm, part_hbm, buck_hbm, counts_hbm, out_ref,
    feats_v, w_v, part_v, buck_v, counts_v, feats_t, e_all, a_all, b_all, meta, recips,
    normed_s, inv_s, own_w, own_part, own_valid, tot_s, g_s, size,
    core_send, core_recv, keep2, send2, recv2, send3, recv3, send4, recv4,
    in_sem, small_sem, out_sem, e_sem, r_sem, c_sem, r2_sem, r3_sem, r4_sem,
):
    dp = lax.axis_index("dp")
    pool = lax.axis_index("pool")
    y = dp // 4
    zh = (dp // 2) % 2
    core = dp % 2
    x = pool // 4
    z = pool % 4
    zs = [z, z + 1 - 2 * (z % 2), (z + 2) % 4, 3 - z]
    middle = z % 2 + z // 2 == 1
    right = (x + 1) % 4
    left = (x + 3) % 4

    def member(dx, c):
        return ((x + dx) % 4) * 4 + zs[c]

    S_META, S_MIDMETA, S_E, S_MID, S_RECIP, S_CORE, S_TWO, S_THREE, S_FOUR = range(9)

    def remote(src, dst, kind, sem, d, p):
        return pltpu.make_async_remote_copy(
            src_ref=src, dst_ref=dst, send_sem=out_sem.at[kind], recv_sem=sem,
            device_id=(d, p), device_id_type=MESH,
        )

    def landed(ref, sem):
        remote(ref, ref, 0, sem, dp, pool).wait_recv()

    barrier = pltpu.get_barrier_semaphore()

    def greet(d, p):
        pl.semaphore_signal(barrier, inc=1, device_id=(d, p), device_id_type=MESH)

    zz = zh * 4 + z
    for k in (2, 6, 1, 7):
        q = (zz + k) % 8
        greet(y * 4 + (q // 4) * 2 + core, x * 4 + q % 4)
    for k in (2, 1, 3):
        greet(dp, ((x + k) % 4) * 4 + z)
        greet(((y + k) % 4) * 4 + zh * 2 + core, pool)
    greet(y * 4 + zh * 2 + (1 - core), pool)

    for k in range(KC):
        cols = pl.ds(k * KW, KW)
        pltpu.make_async_copy(feats_hbm.at[:, cols], feats_v.at[:, cols], in_sem.at[k]).start()
        pltpu.make_async_copy(w_hbm.at[cols, :], w_v.at[cols, :], in_sem.at[k]).start()
    small = [
        pltpu.make_async_copy(part_hbm, part_v, small_sem.at[0]),
        pltpu.make_async_copy(buck_hbm, buck_v, small_sem.at[1]),
        pltpu.make_async_copy(counts_hbm, counts_v, small_sem.at[2]),
    ]
    for c in small:
        c.start()

    projected = None
    for k in range(KC):
        both = pl.ds(0, 2 * KW)
        pltpu.make_async_copy(w_hbm.at[both, :], w_v.at[both, :], in_sem.at[k]).wait()
        cols = pl.ds(k * KW, KW)
        term = nn(feats_v[:, cols], w_v[cols, :])
        projected = term if projected is None else projected + term
    inv_norm = lax.rsqrt(jnp.sum(projected * projected, axis=1, keepdims=True) + EPS)
    normed = projected * inv_norm
    normed_s[...] = normed
    inv_s[...] = jnp.broadcast_to(inv_norm, (ROWS, 128))
    e_all[pool] = normed.astype(jnp.bfloat16)

    for c in small:
        c.wait()
    cnt = counts_v[dp, pool]
    lane = lax.broadcasted_iota(jnp.int32, (1, ROWS), 1)
    valid = lane < cnt
    part_l = jnp.where(valid, part_v[...], -1).astype(jnp.float32)
    w_l = jnp.where(valid, jnp.exp((buck_v[...].astype(jnp.float32) + 0.5) * 0.25), 0.0)
    meta[pool, 0:1, :] = part_l
    meta[pool, 1:2, :] = w_l

    pl.semaphore_wait(barrier, 11)

    def rows_of(h):
        return pl.ds(h * HALF, HALF)

    def sem_of(dx, c, h):
        if dx == 0:
            return e_sem.at[2 * (c - 1) + h]
        if dx == 2:
            return e_sem.at[6 + h] if c == 0 else e_sem.at[15 + c]
        if c % 2:
            return e_sem.at[14 + c // 2]
        onward = h == (0 if dx == 3 else 1)
        return e_sem.at[(8 if c == 0 else 11) + (1 if not onward else 0 if dx == 3 else 2)]

    def go(dx, c, h, side, middle_only=False):
        slot = member(dx, c)
        if side == "right":
            sem, target = sem_of((dx + 3) % 4, c, h), right * 4 + z
        elif side == "left":
            sem, target = sem_of((dx + 1) % 4, c, h), left * 4 + z
        else:
            sem, target = sem_of(dx, c ^ side, h), x * 4 + zs[side]
        half = e_all.at[slot, rows_of(h)]
        remote(half, half, S_MID if middle_only else S_E, sem, dp, target).start()
        if h:
            remote(
                meta.at[slot], meta.at[slot], S_MIDMETA if middle_only else S_META, sem, dp, target
            ).start()

    def arrive(dx, c, h):
        landed(size.at[0:32 + h], sem_of(dx, c, h))

    for h in (0, 1):
        go(0, 0, h, "right")
        go(0, 0, 1 - h, "left")
        go(0, 0, h, 1)

    @pl.when(jnp.logical_not(middle))
    def _():
        for h in (0, 1):
            go(0, 0, h, 2)

    own_part[...] = jnp.broadcast_to(part_l, (128, ROWS)).T
    own_w[...] = jnp.broadcast_to(w_l, (128, ROWS)).T
    own_valid[...] = jnp.broadcast_to(jnp.where(valid, 1.0, 0.0), (128, ROWS)).T

    def wide(v):
        return jnp.concatenate([v, v], axis=1)

    def scores(dx, c):
        slot = member(dx, c)
        s = nt(e_all[pool], e_all[slot])
        e = jnp.exp2(s * SCALE)
        if (dx, c) == (0, 0):
            ri = lax.broadcasted_iota(jnp.int32, (ROWS, ROWS), 0)
            ci = lax.broadcasted_iota(jnp.int32, (ROWS, ROWS), 1)
            e = jnp.where(ri == ci, 0.0, e)
        b_all[slot] = e * wide(own_w[...])
        t = e * meta[slot, 1:2, :]
        a_all[slot] = t
        t = t[:, :128] + t[:, 128:]
        if (dx, c) == (0, 0):
            tot_s[...] = t
        else:
            tot_s[...] += t

    scores(0, 0)

    def transposes(lo, hi):
        for m in range(lo, hi):
            my, mz, mc = m // 4, (m // 2) % 2, m % 2
            t = feats_v[:, m * 128:(m + 1) * 128].T
            which = (mc + core) % 2
            for mx in range(4):
                at = (my * (2 + 6 * mc) + mx * (8 - 6 * mc) + mz) * 32
                feats_t[which, at:at + 32, :] = t[mx * 32:(mx + 1) * 32]

    transposes(0, 16)

    @pl.when(middle)
    def _():
        go(0, 0, 0, 2)

    def spread(c):
        for h in (0, 1):
            arrive(0, c, h)
            go(0, c, h, "right")
            go(0, c, h, "left")

    def rest(c):
        landed(size.at[0:65], sem_of(3, c, 1))
        scores(3, c)
        scores(1, c)

    arrive(3, 0, 0)
    go(3, 0, 0, "right")

    @pl.when(middle)
    def _():
        go(0, 0, 1, 2)

    arrive(1, 0, 1)
    go(1, 0, 1, "left")
    spread(1)

    def send_second(relay):
        for h in (0, 1):
            arrive(0, 2, h)
            if relay:
                go(0, 2, h, 1, True)
            go(0, 2, h, "right")
            go(0, 2, h, "left")

    def send_across():
        for h in (0, 1):
            arrive(2, 0, h)
            go(2, 0, h, 1)
            go(2, 0, h, 3)

    @pl.when(middle)
    def _():
        send_second(True)
        for h in (0, 1):
            go(0, 0, h, 3, True)
        send_across()

    @pl.when(jnp.logical_not(middle))
    def _():
        send_across()
        send_second(False)

    scores(0, 1)
    rest(0)
    scores(2, 0)
    scores(0, 2)
    landed(size.at[0:130], sem_of(3, 1, 0))
    scores(3, 1)
    scores(1, 1)
    arrive(3, 2, 0)
    go(3, 2, 0, "right")
    arrive(1, 2, 1)
    go(1, 2, 1, "left")
    spread(3)
    scores(0, 3)
    rest(2)
    for c in (1, 2, 3):
        landed(size.at[0:65], sem_of(2, c, 0))
        scores(2, c)
    landed(size.at[0:130], sem_of(3, 3, 0))
    scores(3, 3)
    scores(1, 3)

    near = [
        [(0, 0), (0, 1), (1, 0), (3, 0)],
        [(0, 2), (0, 3), (1, 1), (3, 1)],
        [(2, 0), (1, 2), (3, 2), (1, 3), (3, 3), (2, 1)],
        [(2, 2), (2, 3)],
    ]
    total = jnp.broadcast_to(jnp.sum(tot_s[...], axis=1, keepdims=True), (ROWS, 128))
    recip_own = own_valid[...] / total
    recips[pool] = recip_own.T[0:1, :]
    for n, group in reversed(list(enumerate(near))):
        for dx, c in reversed(group):
            if (dx, c) != (0, 0):
                remote(recips.at[pool], recips.at[pool], S_RECIP, r_sem.at[n], dp, member(dx, c)).start()

    tot_s[...] = recip_own
    g_s[...] = jnp.zeros_like(g_s)
    lane_f = lax.broadcasted_iota(jnp.int32, (1, ROWS), 1).astype(jnp.float32)

    def row_term(i, carry):
        acc = None
        for j in range(4):
            s = i * 4 + j
            hit = wide(own_part[...]) == lane_f + (s * ROWS).astype(jnp.float32)
            coef = a_all[s] * wide(tot_s[...])
            coef = jnp.where(hit, coef - 1.0, coef).astype(jnp.bfloat16)
            term = nn(coef, e_all[s])
            acc = term if acc is None else acc + term
        g_s[...] += acc
        return carry

    lax.fori_loop(0, 4, row_term, 0)

    mine = lax.broadcasted_iota(jnp.int32, (ROWS, 128), 0).astype(jnp.float32) + (pool * ROWS).astype(jnp.float32)
    own_part[...] = mine
    for n, group in enumerate(near):
        landed(recips.at[0:len(group) - (n == 0)], r_sem.at[n])
        acc = None
        for dx, c in group:
            s = member(dx, c)
            hit = wide(own_part[...]) == meta[s, 0:1, :]
            coef = b_all[s] * recips[s]
            coef = jnp.where(hit, coef - 1.0, coef).astype(jnp.bfloat16)
            term = nn(coef, e_all[s])
            acc = term if acc is None else acc + term
        g_s[...] += acc

    g = g_s[...]
    nrm = normed_s[...]
    g = (g - nrm * jnp.sum(nrm * g, axis=1, keepdims=True)) * wide(inv_s[...])
    gp = g.astype(jnp.bfloat16)

    a_own = y * (1 - core) + x * core
    b_own = x * (1 - core) + y * core
    turns = (2, 1, 3, 0)
    for t in turns:
        b = (a_own + t) % 4
        core_send[b] = nn(feats_t[1, pl.ds(pl.multiple_of(b * 256, 256), 256), :], gp).astype(core_send.dtype)
        remote(
            core_send.at[b], core_recv.at[b], S_CORE, c_sem.at[b], y * 4 + zh * 2 + (1 - core), pool
        ).start()
    for t in turns:
        b = (b_own + t) % 4
        own = nn(feats_t[0, pl.ds(pl.multiple_of(b * 256, 256), 256), :], gp)
        landed(core_recv.at[b], c_sem.at[b])
        own = own + core_recv[b].astype(jnp.float32)
        for q in range(4):
            keep2[b, q] = own[q * 64:(q + 1) * 64]
            send2[b, q] = own[q * 64:(q + 1) * 64].astype(send2.dtype)
        for u in (2, 1, 3):
            a = (a_own + u) % 4
            ty = a * (1 - core) + y * core
            tx = x * (1 - core) + a * core
            remote(
                send2.at[b, a], recv2.at[b, a_own], S_TWO, r2_sem.at[b], ty * 4 + zh * 2 + core, tx * 4 + z
            ).start()
    for t in turns:
        b = (b_own + t) % 4
        part = keep2[b, a_own]
        landed(recv2.at[b, 0:3], r2_sem.at[b])
        for u in (1, 3, 2):
            part = part + recv2[b, (a_own + u) % 4].astype(jnp.float32)
        if t:
            send3[b] = part.astype(send3.dtype)
            ty = y * (1 - core) + b * core
            tx = b * (1 - core) + x * core
            remote(
                send3.at[b], recv3.at[b_own], S_THREE, r3_sem.at[0], ty * 4 + zh * 2 + core, tx * 4 + z
            ).start()
    landed(recv3.at[0:3], r3_sem.at[0])
    for t in (1, 3, 2):
        part = part + recv3[(b_own + t) % 4].astype(jnp.float32)
    for q in range(8):
        send4[q] = part[q * 8:(q + 1) * 8]
    for t in (4, 3, 5, 2, 6, 1, 7):
        q = (zz + t) % 8
        remote(
            send4.at[q], recv4.at[zz], S_FOUR, r4_sem.at[0], y * 4 + (q // 4) * 2 + core, x * 4 + q % 4
        ).start()
    result = send4[zz]
    landed(recv4.at[0:7], r4_sem.at[0])
    for t in (1, 7, 2, 6, 3, 5, 4):
        result = result + recv4[(zz + t) % 8]
    out_ref[...] = result

    def sent(ref, kind):
        remote(ref, ref, kind, r4_sem.at[0], dp, pool).wait_send()

    sent(meta.at[0:14], S_META)
    pl.when(middle)(lambda: sent(meta.at[0:2], S_MIDMETA))
    sent(e_all.at[0:14], S_E)
    pl.when(middle)(lambda: sent(e_all.at[0:2], S_MID))
    sent(recips.at[0:15], S_RECIP)
    sent(core_send, S_CORE)
    sent(send2.at[0:3], S_TWO)
    sent(send3.at[0:3], S_THREE)
    sent(send4.at[0:7], S_FOUR)


def per_device(feats, tower_w, partners, popularity_buckets, row_counts):
    f32, bf16, i32 = jnp.float32, jnp.bfloat16, jnp.int32
    vmem = pltpu.VMEM
    dma = pltpu.SemaphoreType.DMA
    return pl.pallas_call(
        kernel,
        out_shape=pltpu.VMEM((8, DE), f32),
        in_specs=[pl.BlockSpec(memory_space=pl.ANY)] * 5,
        out_specs=pl.BlockSpec(memory_space=pltpu.VMEM),
        scratch_shapes=[
            vmem((ROWS, DIN), bf16),
            vmem((DIN, DE), bf16),
            vmem((1, ROWS), i32),
            vmem((1, ROWS), i32),
            pltpu.SMEM((16, 16), i32),
            vmem((2, 1024, ROWS), bf16),
            vmem((16, ROWS, DE), bf16),
            vmem((16, ROWS, ROWS), f32),
            vmem((16, ROWS, ROWS), f32),
            vmem((16, 2, ROWS), f32),
            vmem((16, 1, ROWS), f32),
            vmem((ROWS, DE), f32),
            vmem((ROWS, 128), f32),
            vmem((ROWS, 128), f32),
            vmem((ROWS, 128), f32),
            vmem((ROWS, 128), f32),
            vmem((ROWS, 128), f32),
            vmem((ROWS, DE), f32),
            vmem((130, 2, ROWS), f32),
            vmem((4, 256, DE), bf16),
            vmem((4, 256, DE), bf16),
            vmem((4, 4, 64, DE), f32),
            vmem((4, 4, 64, DE), bf16),
            vmem((4, 4, 64, DE), bf16),
            vmem((4, 64, DE), bf16),
            vmem((4, 64, DE), bf16),
            vmem((8, 8, DE), f32),
            vmem((8, 8, DE), f32),
            dma((KC,)),
            dma((3,)),
            dma((9,)),
            dma((19,)),
            dma((4,)),
            dma((4,)),
            dma((4,)),
            dma((1,)),
            dma((1,)),
        ],
        compiler_params=pltpu.CompilerParams(collective_id=0, has_side_effects=True),
    )(feats, tower_w, partners.reshape(1, ROWS), popularity_buckets.reshape(1, ROWS), row_counts)


def solution(mesh):
    return jax.shard_map(
        per_device,
        mesh=mesh,
        in_specs=(P(("dp", "pool"), None), P(), P(("dp", "pool")), P(("dp", "pool")), P()),
        out_specs=P(("dp", "pool"), None),
        check_vma=False,
    )
```

```python
import functools

import jax
import jax.numpy as jnp
from jax import lax
from jax.experimental import pallas as pl
from jax.experimental.pallas import tpu as pltpu
from jax.sharding import PartitionSpec as P

MESH = pl.DeviceIdType.MESH
EPS = 1e-06
SCALE = 28.853900817779268
ROWS = 256
HALF = 128
DE = 256
DIN = 2048
KC = 4
KW = DIN // KC


def by_halves(left, right, contract):
    return jnp.concatenate(
        [
            lax.dot_general(
                left[at:at + HALF], right, (((1,), (contract,)), ((), ())), preferred_element_type=jnp.float32
            )
            for at in range(0, left.shape[0], HALF)
        ],
        axis=0,
    )


def nt(left, right):
    return by_halves(left, right, 1)


def nn(left, right):
    return by_halves(left, right, 0)


def kernel(
    feats_hbm, w_hbm, part_hbm, buck_hbm, counts_hbm, out_ref,
    feats_v, w_v, part_v, buck_v, counts_v, feats_t, e_all, a_all, b_all, meta, recips,
    normed_s, inv_s, own_w, own_part, own_valid, tot_s, g_s, size,
    core_send, core_recv, keep2, send2, recv2, send3, recv3, send4, recv4,
    in_sem, small_sem, out_sem, e_sem, r_sem, c_sem, r2_sem, r3_sem, r4_sem,
):
    dp = lax.axis_index("dp")
    pool = lax.axis_index("pool")
    y = dp // 4
    zh = (dp // 2) % 2
    core = dp % 2
    x = pool // 4
    z = pool % 4
    zs = [z, z + 1 - 2 * (z % 2), (z + 2) % 4, 3 - z]
    middle = z % 2 + z // 2 == 1
    right = (x + 1) % 4
    left = (x + 3) % 4

    def member(dx, c):
        return ((x + dx) % 4) * 4 + zs[c]

    S_META, S_MIDMETA, S_E, S_MID, S_RECIP, S_CORE, S_TWO, S_THREE, S_FOUR = range(9)

    def remote(src, dst, kind, sem, d, p):
        return pltpu.make_async_remote_copy(
            src_ref=src, dst_ref=dst, send_sem=out_sem.at[kind], recv_sem=sem,
            device_id=(d, p), device_id_type=MESH,
        )

    def landed(ref, sem):
        remote(ref, ref, 0, sem, dp, pool).wait_recv()

    barrier = pltpu.get_barrier_semaphore()

    def greet(d, p):
        pl.semaphore_signal(barrier, inc=1, device_id=(d, p), device_id_type=MESH)

    zz = zh * 4 + z
    for k in (2, 6, 1, 7):
        q = (zz + k) % 8
        greet(y * 4 + (q // 4) * 2 + core, x * 4 + q % 4)
    for k in (2, 1, 3):
        greet(dp, ((x + k) % 4) * 4 + z)
        greet(((y + k) % 4) * 4 + zh * 2 + core, pool)
    greet(y * 4 + zh * 2 + (1 - core), pool)

    for k in range(KC):
        cols = pl.ds(k * KW, KW)
        pltpu.make_async_copy(feats_hbm.at[:, cols], feats_v.at[:, cols], in_sem.at[k]).start()
        pltpu.make_async_copy(w_hbm.at[cols, :], w_v.at[cols, :], in_sem.at[k]).start()
    small = [
        pltpu.make_async_copy(part_hbm, part_v, small_sem.at[0]),
        pltpu.make_async_copy(buck_hbm, buck_v, small_sem.at[1]),
        pltpu.make_async_copy(counts_hbm, counts_v, small_sem.at[2]),
    ]
    for c in small:
        c.start()

    projected = None
    for k in range(KC):
        both = pl.ds(0, 2 * KW)
        pltpu.make_async_copy(w_hbm.at[both, :], w_v.at[both, :], in_sem.at[k]).wait()
        cols = pl.ds(k * KW, KW)
        term = nn(feats_v[:, cols], w_v[cols, :])
        projected = term if projected is None else projected + term
    inv_norm = lax.rsqrt(jnp.sum(projected * projected, axis=1, keepdims=True) + EPS)
    normed = projected * inv_norm
    normed_s[...] = normed
    inv_s[...] = jnp.broadcast_to(inv_norm, (ROWS, 128))
    e_all[pool] = normed.astype(jnp.bfloat16)

    for c in small:
        c.wait()
    cnt = counts_v[dp, pool]
    lane = lax.broadcasted_iota(jnp.int32, (1, ROWS), 1)
    valid = lane < cnt
    part_l = jnp.where(valid, part_v[...], -1).astype(jnp.float32)
    w_l = jnp.where(valid, jnp.exp((buck_v[...].astype(jnp.float32) + 0.5) * 0.25), 0.0)
    meta[pool, 0:1, :] = part_l
    meta[pool, 1:2, :] = w_l

    pl.semaphore_wait(barrier, 11)

    def rows_of(h):
        return pl.ds(h * HALF, HALF)

    def sem_of(dx, c, h):
        if dx == 0:
            return e_sem.at[2 * (c - 1) + h]
        if dx == 2:
            return e_sem.at[6 + h] if c == 0 else e_sem.at[15 + c]
        if c % 2:
            return e_sem.at[14 + c // 2]
        onward = h == (0 if dx == 3 else 1)
        return e_sem.at[(8 if c == 0 else 11) + (1 if not onward else 0 if dx == 3 else 2)]

    def go(dx, c, h, side, middle_only=False):
        slot = member(dx, c)
        if side == "right":
            sem, target = sem_of((dx + 3) % 4, c, h), right * 4 + z
        elif side == "left":
            sem, target = sem_of((dx + 1) % 4, c, h), left * 4 + z
        else:
            sem, target = sem_of(dx, c ^ side, h), x * 4 + zs[side]
        half = e_all.at[slot, rows_of(h)]
        remote(half, half, S_MID if middle_only else S_E, sem, dp, target).start()
        if h:
            remote(
                meta.at[slot], meta.at[slot], S_MIDMETA if middle_only else S_META, sem, dp, target
            ).start()

    def arrive(dx, c, h):
        landed(size.at[0:32 + h], sem_of(dx, c, h))

    for h in (0, 1):
        go(0, 0, h, "right")
        go(0, 0, 1 - h, "left")
        go(0, 0, h, 1)

    @pl.when(jnp.logical_not(middle))
    def _():
        for h in (0, 1):
            go(0, 0, h, 2)

    own_part[...] = jnp.broadcast_to(part_l, (128, ROWS)).T
    own_w[...] = jnp.broadcast_to(w_l, (128, ROWS)).T
    own_valid[...] = jnp.broadcast_to(jnp.where(valid, 1.0, 0.0), (128, ROWS)).T

    def wide(v):
        return jnp.concatenate([v, v], axis=1)

    def scores(dx, c):
        slot = member(dx, c)
        s = nt(e_all[pool], e_all[slot])
        e = jnp.exp2(s * SCALE)
        if (dx, c) == (0, 0):
            ri = lax.broadcasted_iota(jnp.int32, (ROWS, ROWS), 0)
            ci = lax.broadcasted_iota(jnp.int32, (ROWS, ROWS), 1)
            e = jnp.where(ri == ci, 0.0, e)
        b_all[slot] = e * wide(own_w[...])
        t = e * meta[slot, 1:2, :]
        a_all[slot] = t
        t = t[:, :128] + t[:, 128:]
        if (dx, c) == (0, 0):
            tot_s[...] = t
        else:
            tot_s[...] += t

    scores(0, 0)

    def transposes(lo, hi):
        for m in range(lo, hi):
            my, mz, mc = m // 4, (m // 2) % 2, m % 2
            t = feats_v[:, m * 128:(m + 1) * 128].T
            which = (mc + core) % 2
            for mx in range(4):
                at = (my * (2 + 6 * mc) + mx * (8 - 6 * mc) + mz) * 32
                feats_t[which, at:at + 32, :] = t[mx * 32:(mx + 1) * 32]

    transposes(0, 16)

    @pl.when(middle)
    def _():
        go(0, 0, 0, 2)

    def spread(c):
        for h in (0, 1):
            arrive(0, c, h)
            go(0, c, h, "right")
            go(0, c, h, "left")

    def rest(c):
        landed(size.at[0:65], sem_of(3, c, 1))
        scores(3, c)
        scores(1, c)

    arrive(3, 0, 0)
    go(3, 0, 0, "right")

    @pl.when(middle)
    def _():
        go(0, 0, 1, 2)

    arrive(1, 0, 1)
    go(1, 0, 1, "left")
    spread(1)

    def send_second(relay):
        for h in (0, 1):
            arrive(0, 2, h)
            if relay:
                go(0, 2, h, 1, True)
            go(0, 2, h, "right")
            go(0, 2, h, "left")

    def send_across():
        for h in (0, 1):
            arrive(2, 0, h)
            go(2, 0, h, 1)
            go(2, 0, h, 3)

    @pl.when(middle)
    def _():
        send_second(True)
        for h in (0, 1):
            go(0, 0, h, 3, True)
        send_across()

    @pl.when(jnp.logical_not(middle))
    def _():
        send_across()
        send_second(False)

    scores(0, 1)
    rest(0)
    scores(2, 0)
    scores(0, 2)
    landed(size.at[0:130], sem_of(3, 1, 0))
    scores(3, 1)
    scores(1, 1)
    arrive(3, 2, 0)
    go(3, 2, 0, "right")
    arrive(1, 2, 1)
    go(1, 2, 1, "left")
    spread(3)
    scores(0, 3)
    rest(2)
    for c in (1, 2, 3):
        landed(size.at[0:65], sem_of(2, c, 0))
        scores(2, c)
    landed(size.at[0:130], sem_of(3, 3, 0))
    scores(3, 3)
    scores(1, 3)

    near = [
        [(0, 0), (0, 1), (1, 0), (3, 0)],
        [(0, 2), (0, 3), (1, 1), (3, 1)],
        [(2, 0), (1, 2), (3, 2), (1, 3), (3, 3), (2, 1)],
        [(2, 2), (2, 3)],
    ]
    by_lane = jnp.sum(tot_s[...].T, axis=0, keepdims=True)
    recips[pool] = jnp.where(meta[pool, 1:2, :] > 0.0, 1.0, 0.0) / by_lane
    for n, group in reversed(list(enumerate(near))):
        for dx, c in reversed(group):
            if (dx, c) != (0, 0):
                remote(recips.at[pool], recips.at[pool], S_RECIP, r_sem.at[n], dp, member(dx, c)).start()

    total = jnp.broadcast_to(jnp.sum(tot_s[...], axis=1, keepdims=True), (ROWS, 128))
    tot_s[...] = own_valid[...] / total
    g_s[...] = jnp.zeros_like(g_s)
    lane_f = lax.broadcasted_iota(jnp.int32, (1, ROWS), 1).astype(jnp.float32)

    def row_term(i, carry):
        acc = None
        for j in range(4):
            s = i * 4 + j
            hit = wide(own_part[...]) == lane_f + (s * ROWS).astype(jnp.float32)
            coef = a_all[s] * wide(tot_s[...])
            coef = jnp.where(hit, coef - 1.0, coef).astype(jnp.bfloat16)
            term = nn(coef, e_all[s])
            acc = term if acc is None else acc + term
        g_s[...] += acc
        return carry

    lax.fori_loop(0, 4, row_term, 0)

    mine = lax.broadcasted_iota(jnp.int32, (ROWS, 128), 0).astype(jnp.float32) + (pool * ROWS).astype(jnp.float32)
    own_part[...] = mine
    for n, group in enumerate(near):
        landed(recips.at[0:len(group) - (n == 0)], r_sem.at[n])
        acc = None
        for dx, c in group:
            s = member(dx, c)
            hit = wide(own_part[...]) == meta[s, 0:1, :]
            coef = b_all[s] * recips[s]
            coef = jnp.where(hit, coef - 1.0, coef).astype(jnp.bfloat16)
            term = nn(coef, e_all[s])
            acc = term if acc is None else acc + term
        g_s[...] += acc

    g = g_s[...]
    nrm = normed_s[...]
    g = (g - nrm * jnp.sum(nrm * g, axis=1, keepdims=True)) * wide(inv_s[...])
    gp = g.astype(jnp.bfloat16)

    a_own = y * (1 - core) + x * core
    b_own = x * (1 - core) + y * core
    turns = (2, 1, 3, 0)
    for t in turns:
        b = (a_own + t) % 4
        core_send[b] = nn(feats_t[1, pl.ds(pl.multiple_of(b * 256, 256), 256), :], gp).astype(core_send.dtype)
        remote(
            core_send.at[b], core_recv.at[b], S_CORE, c_sem.at[b], y * 4 + zh * 2 + (1 - core), pool
        ).start()
    for t in turns:
        b = (b_own + t) % 4
        own = nn(feats_t[0, pl.ds(pl.multiple_of(b * 256, 256), 256), :], gp)
        landed(core_recv.at[b], c_sem.at[b])
        own = own + core_recv[b].astype(jnp.float32)
        for q in range(4):
            keep2[b, q] = own[q * 64:(q + 1) * 64]
            send2[b, q] = own[q * 64:(q + 1) * 64].astype(send2.dtype)
        for u in (2, 1, 3):
            a = (a_own + u) % 4
            ty = a * (1 - core) + y * core
            tx = x * (1 - core) + a * core
            remote(
                send2.at[b, a], recv2.at[b, a_own], S_TWO, r2_sem.at[b], ty * 4 + zh * 2 + core, tx * 4 + z
            ).start()
    for t in turns:
        b = (b_own + t) % 4
        part = keep2[b, a_own]
        landed(recv2.at[b, 0:3], r2_sem.at[b])
        for u in (1, 3, 2):
            part = part + recv2[b, (a_own + u) % 4].astype(jnp.float32)
        if t:
            send3[b] = part.astype(send3.dtype)
            ty = y * (1 - core) + b * core
            tx = b * (1 - core) + x * core
            remote(
                send3.at[b], recv3.at[b_own], S_THREE, r3_sem.at[0], ty * 4 + zh * 2 + core, tx * 4 + z
            ).start()
    landed(recv3.at[0:3], r3_sem.at[0])
    for t in (1, 3, 2):
        part = part + recv3[(b_own + t) % 4].astype(jnp.float32)
    for q in range(8):
        send4[q] = part[q * 8:(q + 1) * 8]
    for t in (4, 3, 5, 2, 6, 1, 7):
        q = (zz + t) % 8
        remote(
            send4.at[q], recv4.at[zz], S_FOUR, r4_sem.at[0], y * 4 + (q // 4) * 2 + core, x * 4 + q % 4
        ).start()
    result = send4[zz]
    landed(recv4.at[0:7], r4_sem.at[0])
    for t in (1, 7, 2, 6, 3, 5, 4):
        result = result + recv4[(zz + t) % 8]
    out_ref[...] = result

    def sent(ref, kind):
        remote(ref, ref, kind, r4_sem.at[0], dp, pool).wait_send()

    sent(meta.at[0:14], S_META)
    pl.when(middle)(lambda: sent(meta.at[0:2], S_MIDMETA))
    sent(e_all.at[0:14], S_E)
    pl.when(middle)(lambda: sent(e_all.at[0:2], S_MID))
    sent(recips.at[0:15], S_RECIP)
    sent(core_send, S_CORE)
    sent(send2.at[0:3], S_TWO)
    sent(send3.at[0:3], S_THREE)
    sent(send4.at[0:7], S_FOUR)


def per_device(feats, tower_w, partners, popularity_buckets, row_counts):
    f32, bf16, i32 = jnp.float32, jnp.bfloat16, jnp.int32
    vmem = pltpu.VMEM
    dma = pltpu.SemaphoreType.DMA
    return pl.pallas_call(
        kernel,
        out_shape=pltpu.VMEM((8, DE), f32),
        in_specs=[pl.BlockSpec(memory_space=pl.ANY)] * 5,
        out_specs=pl.BlockSpec(memory_space=pltpu.VMEM),
        scratch_shapes=[
            vmem((ROWS, DIN), bf16),
            vmem((DIN, DE), bf16),
            vmem((1, ROWS), i32),
            vmem((1, ROWS), i32),
            pltpu.SMEM((16, 16), i32),
            vmem((2, 1024, ROWS), bf16),
            vmem((16, ROWS, DE), bf16),
            vmem((16, ROWS, ROWS), f32),
            vmem((16, ROWS, ROWS), f32),
            vmem((16, 2, ROWS), f32),
            vmem((16, 1, ROWS), f32),
            vmem((ROWS, DE), f32),
            vmem((ROWS, 128), f32),
            vmem((ROWS, 128), f32),
            vmem((ROWS, 128), f32),
            vmem((ROWS, 128), f32),
            vmem((ROWS, 128), f32),
            vmem((ROWS, DE), f32),
            vmem((130, 2, ROWS), f32),
            vmem((4, 256, DE), bf16),
            vmem((4, 256, DE), bf16),
            vmem((4, 4, 64, DE), f32),
            vmem((4, 4, 64, DE), bf16),
            vmem((4, 4, 64, DE), bf16),
            vmem((4, 64, DE), bf16),
            vmem((4, 64, DE), bf16),
            vmem((8, 8, DE), f32),
            vmem((8, 8, DE), f32),
            dma((KC,)),
            dma((3,)),
            dma((9,)),
            dma((19,)),
            dma((4,)),
            dma((4,)),
            dma((4,)),
            dma((1,)),
            dma((1,)),
        ],
        compiler_params=pltpu.CompilerParams(collective_id=0, has_side_effects=True),
    )(feats, tower_w, partners.reshape(1, ROWS), popularity_buckets.reshape(1, ROWS), row_counts)


def solution(mesh):
    return jax.shard_map(
        per_device,
        mesh=mesh,
        in_specs=(P(("dp", "pool"), None), P(), P(("dp", "pool")), P(("dp", "pool")), P()),
        out_specs=P(("dp", "pool"), None),
        check_vma=False,
    )
```

```python
import functools

import jax
import jax.numpy as jnp
from jax import lax
from jax.experimental import pallas as pl
from jax.experimental.pallas import tpu as pltpu
from jax.sharding import PartitionSpec as P

MESH = pl.DeviceIdType.MESH
EPS = 1e-06
SCALE = 28.853900817779268
ROWS = 256
HALF = 128
DE = 256
DIN = 2048
KC = 4
KW = DIN // KC


def by_halves(left, right, contract):
    return jnp.concatenate(
        [
            lax.dot_general(
                left[at:at + HALF], right, (((1,), (contract,)), ((), ())), preferred_element_type=jnp.float32
            )
            for at in range(0, left.shape[0], HALF)
        ],
        axis=0,
    )


def nt(left, right):
    return by_halves(left, right, 1)


def nn(left, right):
    return by_halves(left, right, 0)


def kernel(
    feats_hbm, w_hbm, part_hbm, buck_hbm, counts_hbm, out_ref,
    feats_v, w_v, part_v, buck_v, counts_v, feats_t, e_all, a_all, b_all, meta, recips,
    normed_s, inv_s, own_w, own_part, own_valid, tot_s, g_s, size,
    core_send, core_recv, keep2, send2, recv2, send3, recv3, send4, recv4,
    in_sem, small_sem, out_sem, e_sem, r_sem, c_sem, r2_sem, r3_sem, r4_sem,
):
    dp = lax.axis_index("dp")
    pool = lax.axis_index("pool")
    y = dp // 4
    zh = (dp // 2) % 2
    core = dp % 2
    x = pool // 4
    z = pool % 4
    zs = [z, z + 1 - 2 * (z % 2), (z + 2) % 4, 3 - z]
    middle = z % 2 + z // 2 == 1
    right = (x + 1) % 4
    left = (x + 3) % 4

    def member(dx, c):
        return ((x + dx) % 4) * 4 + zs[c]

    S_META = S_E = S_RECIP = S_CORE = S_TWO = S_THREE = S_FOUR = 0
    S_MID = S_MIDMETA = 1

    def remote(src, dst, kind, sem, d, p):
        return pltpu.make_async_remote_copy(
            src_ref=src, dst_ref=dst, send_sem=out_sem.at[kind], recv_sem=sem,
            device_id=(d, p), device_id_type=MESH,
        )

    def landed(ref, sem):
        remote(ref, ref, 0, sem, dp, pool).wait_recv()

    barrier = pltpu.get_barrier_semaphore()

    def greet(d, p):
        pl.semaphore_signal(barrier, inc=1, device_id=(d, p), device_id_type=MESH)

    zz = zh * 4 + z
    for k in (2, 6, 1, 7):
        q = (zz + k) % 8
        greet(y * 4 + (q // 4) * 2 + core, x * 4 + q % 4)
    for k in (2, 1, 3):
        greet(dp, ((x + k) % 4) * 4 + z)
        greet(((y + k) % 4) * 4 + zh * 2 + core, pool)
    greet(y * 4 + zh * 2 + (1 - core), pool)

    for k in range(KC):
        cols = pl.ds(k * KW, KW)
        pltpu.make_async_copy(feats_hbm.at[:, cols], feats_v.at[:, cols], in_sem.at[k]).start()
        pltpu.make_async_copy(w_hbm.at[cols, :], w_v.at[cols, :], in_sem.at[k]).start()
    small = [
        pltpu.make_async_copy(part_hbm, part_v, small_sem.at[0]),
        pltpu.make_async_copy(buck_hbm, buck_v, small_sem.at[1]),
        pltpu.make_async_copy(counts_hbm, counts_v, small_sem.at[2]),
    ]
    for c in small:
        c.start()

    projected = None
    for k in range(KC):
        both = pl.ds(0, 2 * KW)
        pltpu.make_async_copy(w_hbm.at[both, :], w_v.at[both, :], in_sem.at[k]).wait()
        cols = pl.ds(k * KW, KW)
        term = nn(feats_v[:, cols], w_v[cols, :])
        projected = term if projected is None else projected + term
    inv_norm = lax.rsqrt(jnp.sum(projected * projected, axis=1, keepdims=True) + EPS)
    normed = projected * inv_norm
    normed_s[...] = normed
    inv_s[...] = jnp.broadcast_to(inv_norm, (ROWS, 128))
    e_all[pool] = normed.astype(jnp.bfloat16)

    for c in small:
        c.wait()
    cnt = counts_v[dp, pool]
    lane = lax.broadcasted_iota(jnp.int32, (1, ROWS), 1)
    valid = lane < cnt
    part_l = jnp.where(valid, part_v[...], -1).astype(jnp.float32)
    w_l = jnp.where(valid, jnp.exp((buck_v[...].astype(jnp.float32) + 0.5) * 0.25), 0.0)
    meta[pool, 0:1, :] = part_l
    meta[pool, 1:2, :] = w_l

    pl.semaphore_wait(barrier, 11)

    def rows_of(h):
        return pl.ds(h * HALF, HALF)

    def sem_of(dx, c, h):
        if dx == 0:
            return e_sem.at[2 * (c - 1) + h]
        if dx == 2:
            return e_sem.at[6 + h] if c == 0 else e_sem.at[15 + c]
        if c % 2:
            return e_sem.at[14 + c // 2]
        onward = h == (0 if dx == 3 else 1)
        return e_sem.at[(8 if c == 0 else 11) + (1 if not onward else 0 if dx == 3 else 2)]

    def go(dx, c, h, side, middle_only=False):
        slot = member(dx, c)
        if side == "right":
            sem, target = sem_of((dx + 3) % 4, c, h), right * 4 + z
        elif side == "left":
            sem, target = sem_of((dx + 1) % 4, c, h), left * 4 + z
        else:
            sem, target = sem_of(dx, c ^ side, h), x * 4 + zs[side]
        half = e_all.at[slot, rows_of(h)]
        remote(half, half, S_MID if middle_only else S_E, sem, dp, target).start()
        if h:
            remote(
                meta.at[slot], meta.at[slot], S_MIDMETA if middle_only else S_META, sem, dp, target
            ).start()

    def arrive(dx, c, h):
        landed(size.at[0:64 + 2 * h], sem_of(dx, c, h))

    for h in (0, 1):
        go(0, 0, h, "right")
        go(0, 0, 1 - h, "left")
        go(0, 0, h, 1)

    @pl.when(jnp.logical_not(middle))
    def _():
        for h in (0, 1):
            go(0, 0, h, 2)

    own_part[...] = jnp.broadcast_to(part_l, (128, ROWS)).T
    own_w[...] = jnp.broadcast_to(w_l, (128, ROWS)).T
    own_valid[...] = jnp.broadcast_to(jnp.where(valid, 1.0, 0.0), (128, ROWS)).T

    def wide(v):
        return jnp.concatenate([v, v], axis=1)

    def scores(dx, c):
        slot = member(dx, c)
        s = nt(e_all[pool], e_all[slot])
        e = jnp.exp2(s * SCALE)
        if (dx, c) == (0, 0):
            ri = lax.broadcasted_iota(jnp.int32, (ROWS, ROWS), 0)
            ci = lax.broadcasted_iota(jnp.int32, (ROWS, ROWS), 1)
            e = jnp.where(ri == ci, 0.0, e)
        b_all[slot] = e * wide(own_w[...])
        t = e * meta[slot, 1:2, :]
        a_all[slot] = t
        t = t[:, :128] + t[:, 128:]
        if (dx, c) == (0, 0):
            tot_s[...] = t
        else:
            tot_s[...] += t

    scores(0, 0)

    def transposes(lo, hi):
        for m in range(lo, hi):
            my, mz, mc = m // 4, (m // 2) % 2, m % 2
            t = feats_v[:, m * 128:(m + 1) * 128].T
            which = (mc + core) % 2
            for mx in range(4):
                at = (my * (2 + 6 * mc) + mx * (8 - 6 * mc) + mz) * 32
                feats_t[which, at:at + 32, :] = t[mx * 32:(mx + 1) * 32]

    transposes(0, 16)

    @pl.when(middle)
    def _():
        go(0, 0, 0, 2)

    def spread(c):
        for h in (0, 1):
            arrive(0, c, h)
            go(0, c, h, "right")
            go(0, c, h, "left")

    def rest(c):
        landed(size.at[0:130], sem_of(3, c, 1))
        scores(3, c)
        scores(1, c)

    arrive(3, 0, 0)
    go(3, 0, 0, "right")

    @pl.when(middle)
    def _():
        go(0, 0, 1, 2)

    arrive(1, 0, 1)
    go(1, 0, 1, "left")
    spread(1)

    def send_second(relay):
        for h in (0, 1):
            arrive(0, 2, h)
            if relay:
                go(0, 2, h, 1, True)
            go(0, 2, h, "right")
            go(0, 2, h, "left")

    def send_across():
        for h in (0, 1):
            arrive(2, 0, h)
            go(2, 0, h, 1)
            go(2, 0, h, 3)

    @pl.when(middle)
    def _():
        send_second(True)
        for h in (0, 1):
            go(0, 0, h, 3, True)
        send_across()

    @pl.when(jnp.logical_not(middle))
    def _():
        send_across()
        send_second(False)

    scores(0, 1)
    rest(0)
    scores(2, 0)
    scores(0, 2)
    landed(size.at[0:260], sem_of(3, 1, 0))
    scores(3, 1)
    scores(1, 1)
    arrive(3, 2, 0)
    go(3, 2, 0, "right")
    arrive(1, 2, 1)
    go(1, 2, 1, "left")
    spread(3)
    scores(0, 3)
    rest(2)
    for c in (1, 2, 3):
        landed(size.at[0:130], sem_of(2, c, 0))
        scores(2, c)
    landed(size.at[0:260], sem_of(3, 3, 0))
    scores(3, 3)
    scores(1, 3)

    near = [
        [(0, 0), (0, 1), (1, 0), (3, 0)],
        [(0, 2), (0, 3), (1, 1), (3, 1)],
        [(2, 0), (1, 2), (3, 2), (1, 3), (3, 3), (2, 1)],
        [(2, 2), (2, 3)],
    ]
    by_lane = jnp.sum(tot_s[...].T, axis=0, keepdims=True)
    recips[pool] = jnp.where(meta[pool, 1:2, :] > 0.0, 1.0, 0.0) / by_lane
    for n, group in reversed(list(enumerate(near))):
        for dx, c in reversed(group):
            if (dx, c) != (0, 0):
                remote(recips.at[pool], recips.at[pool], S_RECIP, r_sem.at[n], dp, member(dx, c)).start()

    total = jnp.broadcast_to(jnp.sum(tot_s[...], axis=1, keepdims=True), (ROWS, 128))
    tot_s[...] = own_valid[...] / total
    g_s[...] = jnp.zeros_like(g_s)
    lane_f = lax.broadcasted_iota(jnp.int32, (1, ROWS), 1).astype(jnp.float32)

    def row_term(i, carry):
        acc = None
        for j in range(4):
            s = i * 4 + j
            hit = wide(own_part[...]) == lane_f + (s * ROWS).astype(jnp.float32)
            coef = a_all[s] * wide(tot_s[...])
            coef = jnp.where(hit, coef - 1.0, coef).astype(jnp.bfloat16)
            term = nn(coef, e_all[s])
            acc = term if acc is None else acc + term
        g_s[...] += acc
        return carry

    lax.fori_loop(0, 4, row_term, 0)

    mine = lax.broadcasted_iota(jnp.int32, (ROWS, 128), 0).astype(jnp.float32) + (pool * ROWS).astype(jnp.float32)
    own_part[...] = mine
    for n, group in enumerate(near):
        landed(recips.at[0:len(group) - (n == 0)], r_sem.at[n])
        acc = None
        for dx, c in group:
            s = member(dx, c)
            hit = wide(own_part[...]) == meta[s, 0:1, :]
            coef = b_all[s] * recips[s]
            coef = jnp.where(hit, coef - 1.0, coef).astype(jnp.bfloat16)
            term = nn(coef, e_all[s])
            acc = term if acc is None else acc + term
        g_s[...] += acc

    g = g_s[...]
    nrm = normed_s[...]
    g = (g - nrm * jnp.sum(nrm * g, axis=1, keepdims=True)) * wide(inv_s[...])
    gp = g.astype(jnp.bfloat16)

    a_own = y * (1 - core) + x * core
    b_own = x * (1 - core) + y * core
    turns = (2, 1, 3, 0)
    for t in turns:
        b = (a_own + t) % 4
        core_send[b] = nn(feats_t[1, pl.ds(pl.multiple_of(b * 256, 256), 256), :], gp).astype(core_send.dtype)
        remote(
            core_send.at[b], core_recv.at[b], S_CORE, c_sem.at[b], y * 4 + zh * 2 + (1 - core), pool
        ).start()
    for t in turns:
        b = (b_own + t) % 4
        own = nn(feats_t[0, pl.ds(pl.multiple_of(b * 256, 256), 256), :], gp)
        landed(core_recv.at[b], c_sem.at[b])
        own = own + core_recv[b].astype(jnp.float32)
        for q in range(4):
            keep2[b, q] = own[q * 64:(q + 1) * 64]
            send2[b, q] = own[q * 64:(q + 1) * 64].astype(send2.dtype)
        for u in (2, 1, 3):
            a = (a_own + u) % 4
            ty = a * (1 - core) + y * core
            tx = x * (1 - core) + a * core
            remote(
                send2.at[b, a], recv2.at[b, a_own], S_TWO, r2_sem.at[b], ty * 4 + zh * 2 + core, tx * 4 + z
            ).start()
    for t in turns:
        b = (b_own + t) % 4
        part = keep2[b, a_own]
        landed(recv2.at[b, 0:3], r2_sem.at[b])
        for u in (1, 3, 2):
            part = part + recv2[b, (a_own + u) % 4].astype(jnp.float32)
        if t:
            send3[b] = part.astype(send3.dtype)
            ty = y * (1 - core) + b * core
            tx = b * (1 - core) + x * core
            remote(
                send3.at[b], recv3.at[b_own], S_THREE, r3_sem.at[0], ty * 4 + zh * 2 + core, tx * 4 + z
            ).start()
    landed(recv3.at[0:3], r3_sem.at[0])
    for t in (1, 3, 2):
        part = part + recv3[(b_own + t) % 4].astype(jnp.float32)
    for q in range(8):
        send4[q] = part[q * 8:(q + 1) * 8]
    for t in (4, 3, 5, 2, 6, 1, 7):
        q = (zz + t) % 8
        remote(
            send4.at[q], recv4.at[zz], S_FOUR, r4_sem.at[0], y * 4 + (q // 4) * 2 + core, x * 4 + q % 4
        ).start()
    result = send4[zz]
    landed(recv4.at[0:7], r4_sem.at[0])
    for t in (1, 7, 2, 6, 3, 5, 4):
        result = result + recv4[(zz + t) % 8]
    out_ref[...] = result

    def sent(ref, kind):
        remote(ref, ref, kind, r4_sem.at[0], dp, pool).wait_send()

    sent(size.at[0:14 * 128 + 14 * 2 + 15 + 4 * 128 + 12 * 32 + 3 * 32 + 7 * 8], S_E)
    pl.when(middle)(lambda: sent(size.at[0:2 * 128 + 2 * 2], S_MID))


def per_device(feats, tower_w, partners, popularity_buckets, row_counts):
    f32, bf16, i32 = jnp.float32, jnp.bfloat16, jnp.int32
    vmem = pltpu.VMEM
    dma = pltpu.SemaphoreType.DMA
    return pl.pallas_call(
        kernel,
        out_shape=pltpu.VMEM((8, DE), f32),
        in_specs=[pl.BlockSpec(memory_space=pl.ANY)] * 5,
        out_specs=pl.BlockSpec(memory_space=pltpu.VMEM),
        scratch_shapes=[
            vmem((ROWS, DIN), bf16),
            vmem((DIN, DE), bf16),
            vmem((1, ROWS), i32),
            vmem((1, ROWS), i32),
            pltpu.SMEM((16, 16), i32),
            vmem((2, 1024, ROWS), bf16),
            vmem((16, ROWS, DE), bf16),
            vmem((16, ROWS, ROWS), f32),
            vmem((16, ROWS, ROWS), f32),
            vmem((16, 2, ROWS), f32),
            vmem((16, 1, ROWS), f32),
            vmem((ROWS, DE), f32),
            vmem((ROWS, 128), f32),
            vmem((ROWS, 128), f32),
            vmem((ROWS, 128), f32),
            vmem((ROWS, 128), f32),
            vmem((ROWS, 128), f32),
            vmem((ROWS, DE), f32),
            vmem((2883, 1, ROWS), f32),
            vmem((4, 256, DE), bf16),
            vmem((4, 256, DE), bf16),
            vmem((4, 4, 64, DE), f32),
            vmem((4, 4, 64, DE), bf16),
            vmem((4, 4, 64, DE), bf16),
            vmem((4, 64, DE), bf16),
            vmem((4, 64, DE), bf16),
            vmem((8, 8, DE), f32),
            vmem((8, 8, DE), f32),
            dma((KC,)),
            dma((3,)),
            dma((2,)),
            dma((19,)),
            dma((4,)),
            dma((4,)),
            dma((4,)),
            dma((1,)),
            dma((1,)),
        ],
        compiler_params=pltpu.CompilerParams(collective_id=0, has_side_effects=True),
    )(feats, tower_w, partners.reshape(1, ROWS), popularity_buckets.reshape(1, ROWS), row_counts)


def solution(mesh):
    return jax.shard_map(
        per_device,
        mesh=mesh,
        in_specs=(P(("dp", "pool"), None), P(), P(("dp", "pool")), P(("dp", "pool")), P()),
        out_specs=P(("dp", "pool"), None),
        check_vma=False,
    )
```

```python
import functools

import jax
import jax.numpy as jnp
from jax import lax
from jax.experimental import pallas as pl
from jax.experimental.pallas import tpu as pltpu
from jax.sharding import PartitionSpec as P

MESH = pl.DeviceIdType.MESH
EPS = 1e-06
SCALE = 28.853900817779268
ROWS = 256
HALF = 128
DE = 256
DIN = 2048
KC = 4
KW = DIN // KC


def by_halves(left, right, contract):
    return jnp.concatenate(
        [
            lax.dot_general(
                left[at:at + HALF], right, (((1,), (contract,)), ((), ())), preferred_element_type=jnp.float32
            )
            for at in range(0, left.shape[0], HALF)
        ],
        axis=0,
    )


def nt(left, right):
    return by_halves(left, right, 1)


def nn(left, right):
    return by_halves(left, right, 0)


def kernel(
    feats_hbm, w_hbm, part_hbm, buck_hbm, counts_hbm, out_ref,
    feats_v, w_v, part_v, buck_v, counts_v, feats_t, e_all, a_all, b_all, meta, recips,
    normed_s, inv_s, own_w, own_part, own_valid, tot_s, g_s, size,
    core_send, core_recv, keep2, send2, recv2, send3, recv3, send4, recv4,
    in_sem, small_sem, out_sem, e_sem, r_sem, c_sem, r2_sem, r3_sem, r4_sem,
):
    dp = lax.axis_index("dp")
    pool = lax.axis_index("pool")
    y = dp // 4
    zh = (dp // 2) % 2
    core = dp % 2
    x = pool // 4
    z = pool % 4
    zs = [z, z + 1 - 2 * (z % 2), (z + 2) % 4, 3 - z]
    middle = z % 2 + z // 2 == 1
    right = (x + 1) % 4
    left = (x + 3) % 4

    def member(dx, c):
        return ((x + dx) % 4) * 4 + zs[c]

    S_META = S_E = S_RECIP = S_CORE = S_TWO = S_THREE = S_FOUR = 0
    S_MID = S_MIDMETA = 1

    def remote(src, dst, kind, sem, d, p):
        return pltpu.make_async_remote_copy(
            src_ref=src, dst_ref=dst, send_sem=out_sem.at[kind], recv_sem=sem,
            device_id=(d, p), device_id_type=MESH,
        )

    def landed(ref, sem):
        remote(ref, ref, 0, sem, dp, pool).wait_recv()

    barrier = pltpu.get_barrier_semaphore()

    def greet(d, p):
        pl.semaphore_signal(barrier, inc=1, device_id=(d, p), device_id_type=MESH)

    zz = zh * 4 + z
    for k in (2, 6, 1, 7):
        q = (zz + k) % 8
        greet(y * 4 + (q // 4) * 2 + core, x * 4 + q % 4)
    for k in (2, 1, 3):
        greet(dp, ((x + k) % 4) * 4 + z)
        greet(((y + k) % 4) * 4 + zh * 2 + core, pool)
    greet(y * 4 + zh * 2 + (1 - core), pool)

    for k in range(KC):
        cols = pl.ds(k * KW, KW)
        pltpu.make_async_copy(feats_hbm.at[:, cols], feats_v.at[:, cols], in_sem.at[k]).start()
        pltpu.make_async_copy(w_hbm.at[cols, :], w_v.at[cols, :], in_sem.at[k]).start()
    small = [
        pltpu.make_async_copy(part_hbm, part_v, small_sem.at[0]),
        pltpu.make_async_copy(buck_hbm, buck_v, small_sem.at[0]),
        pltpu.make_async_copy(counts_hbm, counts_v, small_sem.at[1]),
    ]
    for c in small:
        c.start()

    projected = None
    for k in range(KC):
        both = pl.ds(0, 2 * KW)
        pltpu.make_async_copy(w_hbm.at[both, :], w_v.at[both, :], in_sem.at[k]).wait()
        cols = pl.ds(k * KW, KW)
        term = nn(feats_v[:, cols], w_v[cols, :])
        projected = term if projected is None else projected + term
    inv_norm = lax.rsqrt(jnp.sum(projected * projected, axis=1, keepdims=True) + EPS)
    normed = projected * inv_norm
    normed_s[...] = normed
    inv_s[...] = jnp.broadcast_to(inv_norm, (ROWS, 128))
    e_all[pool] = normed.astype(jnp.bfloat16)

    pltpu.make_async_copy(size.at[0:2], size.at[0:2], small_sem.at[0]).wait()
    small[2].wait()
    cnt = counts_v[dp, pool]
    lane = lax.broadcasted_iota(jnp.int32, (1, ROWS), 1)
    valid = lane < cnt
    part_l = jnp.where(valid, part_v[...], -1).astype(jnp.float32)
    w_l = jnp.where(valid, jnp.exp((buck_v[...].astype(jnp.float32) + 0.5) * 0.25), 0.0)
    meta[pool, 0:1, :] = part_l
    meta[pool, 1:2, :] = w_l

    pl.semaphore_wait(barrier, 11)

    def rows_of(h):
        return pl.ds(h * HALF, HALF)

    def sem_of(dx, c, h):
        if dx == 0:
            return e_sem.at[2 * (c - 1) + h]
        if dx == 2:
            return e_sem.at[6 + h] if c == 0 else e_sem.at[15 + c]
        if c % 2:
            return e_sem.at[14 + c // 2]
        onward = h == (0 if dx == 3 else 1)
        return e_sem.at[(8 if c == 0 else 11) + (1 if not onward else 0 if dx == 3 else 2)]

    def go(dx, c, h, side, middle_only=False):
        slot = member(dx, c)
        if side == "right":
            sem, target = sem_of((dx + 3) % 4, c, h), right * 4 + z
        elif side == "left":
            sem, target = sem_of((dx + 1) % 4, c, h), left * 4 + z
        else:
            sem, target = sem_of(dx, c ^ side, h), x * 4 + zs[side]
        half = e_all.at[slot, rows_of(h)]
        remote(half, half, S_MID if middle_only else S_E, sem, dp, target).start()
        if h:
            remote(
                meta.at[slot], meta.at[slot], S_MIDMETA if middle_only else S_META, sem, dp, target
            ).start()

    def arrive(dx, c, h):
        landed(size.at[0:64 + 2 * h], sem_of(dx, c, h))

    for h in (0, 1):
        go(0, 0, h, "right")
        go(0, 0, 1 - h, "left")
        go(0, 0, h, 1)

    @pl.when(jnp.logical_not(middle))
    def _():
        for h in (0, 1):
            go(0, 0, h, 2)

    own_part[...] = jnp.broadcast_to(part_l, (128, ROWS)).T
    own_w[...] = jnp.broadcast_to(w_l, (128, ROWS)).T
    own_valid[...] = jnp.broadcast_to(jnp.where(valid, 1.0, 0.0), (128, ROWS)).T

    def wide(v):
        return jnp.concatenate([v, v], axis=1)

    def scores(dx, c):
        slot = member(dx, c)
        s = nt(e_all[pool], e_all[slot])
        e = jnp.exp2(s * SCALE)
        if (dx, c) == (0, 0):
            ri = lax.broadcasted_iota(jnp.int32, (ROWS, ROWS), 0)
            ci = lax.broadcasted_iota(jnp.int32, (ROWS, ROWS), 1)
            e = jnp.where(ri == ci, 0.0, e)
        b_all[slot] = e * wide(own_w[...])
        t = e * meta[slot, 1:2, :]
        a_all[slot] = t
        t = t[:, :128] + t[:, 128:]
        if (dx, c) == (0, 0):
            tot_s[...] = t
        else:
            tot_s[...] += t

    scores(0, 0)

    def transposes(lo, hi):
        for m in range(lo, hi):
            my, mz, mc = m // 4, (m // 2) % 2, m % 2
            t = feats_v[:, m * 128:(m + 1) * 128].T
            which = (mc + core) % 2
            for mx in range(4):
                at = (my * (2 + 6 * mc) + mx * (8 - 6 * mc) + mz) * 32
                feats_t[which, at:at + 32, :] = t[mx * 32:(mx + 1) * 32]

    transposes(0, 16)

    @pl.when(middle)
    def _():
        go(0, 0, 0, 2)

    def spread(c):
        for h in (0, 1):
            arrive(0, c, h)
            go(0, c, h, "right")
            go(0, c, h, "left")

    def rest(c):
        landed(size.at[0:130], sem_of(3, c, 1))
        scores(3, c)
        scores(1, c)

    arrive(3, 0, 0)
    go(3, 0, 0, "right")

    @pl.when(middle)
    def _():
        go(0, 0, 1, 2)

    arrive(1, 0, 1)
    go(1, 0, 1, "left")
    spread(1)

    def send_second(relay):
        for h in (0, 1):
            arrive(0, 2, h)
            if relay:
                go(0, 2, h, 1, True)
            go(0, 2, h, "right")
            go(0, 2, h, "left")

    def send_across():
        for h in (0, 1):
            arrive(2, 0, h)
            go(2, 0, h, 1)
            go(2, 0, h, 3)

    @pl.when(middle)
    def _():
        send_second(True)
        for h in (0, 1):
            go(0, 0, h, 3, True)
        send_across()

    @pl.when(jnp.logical_not(middle))
    def _():
        send_across()
        send_second(False)

    scores(0, 1)
    rest(0)
    scores(2, 0)
    scores(0, 2)
    landed(size.at[0:260], sem_of(3, 1, 0))
    scores(3, 1)
    scores(1, 1)
    arrive(3, 2, 0)
    go(3, 2, 0, "right")
    arrive(1, 2, 1)
    go(1, 2, 1, "left")
    spread(3)
    scores(0, 3)
    rest(2)
    for c in (1, 2, 3):
        landed(size.at[0:130], sem_of(2, c, 0))
        scores(2, c)
    landed(size.at[0:260], sem_of(3, 3, 0))
    scores(3, 3)
    scores(1, 3)

    near = [
        [(0, 0), (0, 1), (1, 0), (3, 0)],
        [(0, 2), (0, 3), (1, 1), (3, 1)],
        [(2, 0), (1, 2), (3, 2), (1, 3), (3, 3), (2, 1)],
        [(2, 2), (2, 3)],
    ]
    by_lane = jnp.sum(tot_s[...].T, axis=0, keepdims=True)
    recips[pool] = jnp.where(meta[pool, 1:2, :] > 0.0, 1.0, 0.0) / by_lane
    for n, group in reversed(list(enumerate(near))):
        for dx, c in reversed(group):
            if (dx, c) != (0, 0):
                remote(recips.at[pool], recips.at[pool], S_RECIP, r_sem.at[n], dp, member(dx, c)).start()

    total = jnp.broadcast_to(jnp.sum(tot_s[...], axis=1, keepdims=True), (ROWS, 128))
    tot_s[...] = own_valid[...] / total
    g_s[...] = jnp.zeros_like(g_s)
    lane_f = lax.broadcasted_iota(jnp.int32, (1, ROWS), 1).astype(jnp.float32)

    def row_term(i, carry):
        acc = None
        for j in range(4):
            s = i * 4 + j
            hit = wide(own_part[...]) == lane_f + (s * ROWS).astype(jnp.float32)
            coef = a_all[s] * wide(tot_s[...])
            coef = jnp.where(hit, coef - 1.0, coef).astype(jnp.bfloat16)
            term = nn(coef, e_all[s])
            acc = term if acc is None else acc + term
        g_s[...] += acc
        return carry

    lax.fori_loop(0, 4, row_term, 0)

    mine = lax.broadcasted_iota(jnp.int32, (ROWS, 128), 0).astype(jnp.float32) + (pool * ROWS).astype(jnp.float32)
    own_part[...] = mine
    for n, group in enumerate(near):
        landed(recips.at[0:len(group) - (n == 0)], r_sem.at[n])
        acc = None
        for dx, c in group:
            s = member(dx, c)
            hit = wide(own_part[...]) == meta[s, 0:1, :]
            coef = b_all[s] * recips[s]
            coef = jnp.where(hit, coef - 1.0, coef).astype(jnp.bfloat16)
            term = nn(coef, e_all[s])
            acc = term if acc is None else acc + term
        g_s[...] += acc

    g = g_s[...]
    nrm = normed_s[...]
    g = (g - nrm * jnp.sum(nrm * g, axis=1, keepdims=True)) * wide(inv_s[...])
    gp = g.astype(jnp.bfloat16)

    a_own = y * (1 - core) + x * core
    b_own = x * (1 - core) + y * core
    turns = (2, 1, 3, 0)
    for t in turns:
        b = (a_own + t) % 4
        core_send[b] = nn(feats_t[1, pl.ds(pl.multiple_of(b * 256, 256), 256), :], gp).astype(core_send.dtype)
        remote(
            core_send.at[b], core_recv.at[b], S_CORE, c_sem.at[b], y * 4 + zh * 2 + (1 - core), pool
        ).start()
    for t in turns:
        b = (b_own + t) % 4
        own = nn(feats_t[0, pl.ds(pl.multiple_of(b * 256, 256), 256), :], gp)
        landed(core_recv.at[b], c_sem.at[b])
        own = own + core_recv[b].astype(jnp.float32)
        for q in range(4):
            keep2[b, q] = own[q * 64:(q + 1) * 64]
            send2[b, q] = own[q * 64:(q + 1) * 64].astype(send2.dtype)
        for u in (2, 1, 3):
            a = (a_own + u) % 4
            ty = a * (1 - core) + y * core
            tx = x * (1 - core) + a * core
            remote(
                send2.at[b, a], recv2.at[b, a_own], S_TWO, r2_sem.at[b], ty * 4 + zh * 2 + core, tx * 4 + z
            ).start()
    for t in turns:
        b = (b_own + t) % 4
        part = keep2[b, a_own]
        landed(recv2.at[b, 0:3], r2_sem.at[b])
        for u in (1, 3, 2):
            part = part + recv2[b, (a_own + u) % 4].astype(jnp.float32)
        if t:
            send3[b] = part.astype(send3.dtype)
            ty = y * (1 - core) + b * core
            tx = b * (1 - core) + x * core
            remote(
                send3.at[b], recv3.at[b_own], S_THREE, r3_sem.at[0], ty * 4 + zh * 2 + core, tx * 4 + z
            ).start()
    landed(recv3.at[0:3], r3_sem.at[0])
    for t in (1, 3, 2):
        part = part + recv3[(b_own + t) % 4].astype(jnp.float32)
    for q in range(8):
        send4[q] = part[q * 8:(q + 1) * 8]
    for t in (4, 3, 5, 2, 6, 1, 7):
        q = (zz + t) % 8
        remote(
            send4.at[q], recv4.at[zz], S_FOUR, r4_sem.at[0], y * 4 + (q // 4) * 2 + core, x * 4 + q % 4
        ).start()
    result = send4[zz]
    landed(recv4.at[0:7], r4_sem.at[0])
    for t in (1, 7, 2, 6, 3, 5, 4):
        result = result + recv4[(zz + t) % 8]
    out_ref[...] = result

    def sent(ref, kind):
        remote(ref, ref, kind, r4_sem.at[0], dp, pool).wait_send()

    sent(size.at[0:14 * 128 + 14 * 2 + 15 + 4 * 128 + 12 * 32 + 3 * 32 + 7 * 8], S_E)
    pl.when(middle)(lambda: sent(size.at[0:2 * 128 + 2 * 2], S_MID))


def per_device(feats, tower_w, partners, popularity_buckets, row_counts):
    f32, bf16, i32 = jnp.float32, jnp.bfloat16, jnp.int32
    vmem = pltpu.VMEM
    dma = pltpu.SemaphoreType.DMA
    return pl.pallas_call(
        kernel,
        out_shape=pltpu.VMEM((8, DE), f32),
        in_specs=[pl.BlockSpec(memory_space=pl.ANY)] * 5,
        out_specs=pl.BlockSpec(memory_space=pltpu.VMEM),
        scratch_shapes=[
            vmem((ROWS, DIN), bf16),
            vmem((DIN, DE), bf16),
            vmem((1, ROWS), i32),
            vmem((1, ROWS), i32),
            pltpu.SMEM((16, 16), i32),
            vmem((2, 1024, ROWS), bf16),
            vmem((16, ROWS, DE), bf16),
            vmem((16, ROWS, ROWS), f32),
            vmem((16, ROWS, ROWS), f32),
            vmem((16, 2, ROWS), f32),
            vmem((16, 1, ROWS), f32),
            vmem((ROWS, DE), f32),
            vmem((ROWS, 128), f32),
            vmem((ROWS, 128), f32),
            vmem((ROWS, 128), f32),
            vmem((ROWS, 128), f32),
            vmem((ROWS, 128), f32),
            vmem((ROWS, DE), f32),
            vmem((2883, 1, ROWS), f32),
            vmem((4, 256, DE), bf16),
            vmem((4, 256, DE), bf16),
            vmem((4, 4, 64, DE), f32),
            vmem((4, 4, 64, DE), bf16),
            vmem((4, 4, 64, DE), bf16),
            vmem((4, 64, DE), bf16),
            vmem((4, 64, DE), bf16),
            vmem((8, 8, DE), f32),
            vmem((8, 8, DE), f32),
            dma((KC,)),
            dma((2,)),
            dma((2,)),
            dma((19,)),
            dma((4,)),
            dma((4,)),
            dma((4,)),
            dma((1,)),
            dma((1,)),
        ],
        compiler_params=pltpu.CompilerParams(collective_id=0, has_side_effects=True),
    )(feats, tower_w, partners.reshape(1, ROWS), popularity_buckets.reshape(1, ROWS), row_counts)


def solution(mesh):
    return jax.shard_map(
        per_device,
        mesh=mesh,
        in_specs=(P(("dp", "pool"), None), P(), P(("dp", "pool")), P(("dp", "pool")), P()),
        out_specs=P(("dp", "pool"), None),
        check_vma=False,
    )
```
